32 devices in a mesh: expert: 2 (over x), dp: 16 (over z, y, core).
Axes of the slice: x: 2, y: 2, z: 4, core: 2. Of those that a mesh axis runs over, the one named last changes fastest.
Arguments:
- tokens: bfloat16 [4096, 3072], P(('expert', 'dp')), may hold values from -6 to 6
- out_grad: bfloat16 [4096, 3072], P(('expert', 'dp')), may hold values from -6 to 6
- routes: int32 [4096, 2], P(('expert', 'dp')), may hold values from 0 to 7, all different within a row; in each aligned block of 128 rows (0 to 127, 128 to 255, ...) at most 40 rows name the same one
- gates: float32 [4096, 2], P(('expert', 'dp')), may hold values from 0.2 to 1
- w_gate: bfloat16 [8, 3072, 128], P('expert', 'dp'), may hold values from -0.109375 to 0.109375
- w_up: bfloat16 [8, 3072, 128], P('expert', 'dp'), may hold values from -0.109375 to 0.109375
- w_down_t: bfloat16 [8, 3072, 128], P('expert', 'dp'), may hold values from -0.5 to 0.5
Outputs:
- token_grad: bfloat16 [4096, 3072], P(('expert', 'dp'))
- grad_gate: float32 [8, 3072, 128], P('expert', 'dp')
- grad_up: float32 [8, 3072, 128], P('expert', 'dp')
The draws below stay inside these ranges and needn't reach their ends.
Inputs may be any that keep to these rules, and one draw needn't show every extreme that they name: `routes`: each row names two different experts. No expert is named by more than 40 of the rows of one device, and in every draw some device names some expert exactly 40 times.
All inputs are finite; a program needn't handle non-finite values.
Results may differ from the reference program's by a relative error of at most 0.0065.
Values may be sent and summed in bfloat16 or wider, within the bound.
A program may use at most 64 MiB of HBM per device.

```python
import math
import jax
import jax.numpy as jnp
import numpy as np
from jax import lax

D = 3072
FF = 128
EXPERTS = 8
TOK_DEV = 128
CAP = 40
TOKENS = 4096
DEVICES = 32


def spiked(array, own_key, source, target, blocks, factor):
    owner, partner = [(jnp.arange(array.shape[position]) // (array.shape[position] // blocks)).reshape([-1 if axis == position else 1 for axis in range(array.ndim)]) for position in (source, target)]
    chosen = jax.random.permutation(own_key, blocks)[partner]
    strong = (owner == chosen) | (owner == (partner + blocks // 2) % blocks)
    return jnp.where(strong, factor * array, array)


def block_scale(key, extent, cuts, least, top_value):
    factor_of, own = 1.0, jax.random.fold_in(key, 6)
    for dim, shards_of in cuts:
        heights = jnp.exp(jax.random.uniform(jax.random.fold_in(own, dim), (shards_of,), jnp.float32, least / len(cuts), top_value / len(cuts)))
        factor_of = factor_of * jnp.repeat(heights, extent[dim] // shards_of).reshape([-1 if axis == dim else 1 for axis in range(len(extent))])
    return factor_of


def deal_out(stream_key, own, number, rows, count, top, bound, skew):
    order = jax.random.permutation(stream_key, count)
    crowded, usual = shares(count, rows * top, bound, skew, True), shares(count, rows * top, bound, skew, False)
    places = jnp.arange(count)

    def named(tallies, rotation):
        used = int((tallies > 0).sum())
        fixed = max(1, used // 4)
        moved = fixed + (places - fixed + rotation * (used - fixed)) % max(1, count - fixed)
        return jnp.zeros((count,), jnp.int32).at[order[jnp.where(places < fixed, places, moved)]].set(jnp.asarray(tallies, jnp.int32))

    tallies = jnp.where(number % 4 == 0, named(crowded, number // 4), named(usual, number - number // 4 - 1))
    mixed = jax.random.permutation(jax.random.fold_in(own, 3), count)
    giver, receiver = mixed[0:count // 2 * 2:2], mixed[1:count // 2 * 2:2]
    slack = jnp.minimum(tallies[giver] - 1, bound - tallies[receiver]) // 2
    slack = jnp.where((giver == order[0]) | (receiver == order[0]) | (tallies[receiver] == 0), 0, jnp.maximum(slack, 0))
    moved = jax.random.randint(jax.random.fold_in(own, 4), (count // 2,), 0, 1 << 20) % (slack + 1)
    tallies = tallies.at[giver].add(-moved).at[receiver].add(moved)
    labels = jnp.searchsorted(jnp.cumsum(tallies), jnp.arange(rows * top), side="right").astype(jnp.int32)
    grid = labels.reshape(top, rows).T
    grid = grid[jax.random.permutation(jax.random.fold_in(own, 1), rows)]
    rotation = jax.random.randint(jax.random.fold_in(own, 2), (rows, 1), 0, top)
    return jnp.take_along_axis(grid, (jnp.arange(top)[None, :] + rotation) % top, axis=1)


def shares(count, total, limit, slope, full):
    weights = [(1 << 20) // math.isqrt(grade ** slope) + 1 for grade in range(1, count + 1)]
    largest = limit if full else min(limit, max(-(-total // count), total * weights[0] // sum(weights)))
    least = 1 if total - largest >= count - 1 else 0
    given, rest = [largest] + [least] * (count - 1), total - largest - least * (count - 1)
    while rest > 0:
        candidates = [i for i in range(1, count) if given[i] < largest] or [i for i in range(1, count) if given[i] < limit]
        pool, left = sum([weights[i] for i in candidates]), rest
        for i in candidates:
            extra = min(limit - given[i], max(1, left * weights[i] // pool), rest)
            given[i] = given[i] + extra
            rest = rest - extra
    return np.array(given)


def normal_values(rng, dims, spread, most, shards=(), held_as=jnp.bfloat16):
    drawn = spread * jax.random.normal(rng, dims, jnp.float32)
    if shards:
        drawn = drawn * block_scale(rng, dims, shards, -0.22, 0.18)
    return jnp.clip(drawn, -most, most).astype(held_as)


def noise_with(stream_key, extent, deviation, most, cuts, heavy, kind=jnp.bfloat16):
    drawn = deviation * jax.random.normal(stream_key, extent, jnp.float32)
    if cuts:
        drawn = drawn * block_scale(stream_key, extent, cuts, -0.22, 0.18)
    return jnp.clip(spiked(drawn, jax.random.fold_in(stream_key, 3), *heavy), -most, most).astype(kind)


def setup_inputs(seed: int = 0) -> dict:
    key_list = jax.random.split(jax.random.key(seed), 8)
    tokens = noise_with(key_list[0], (TOKENS, D), 1.0, 6.0, ((0, 32),), (0, 1, 32, 2.75))
    out_grad = normal_values(key_list[1], (TOKENS, D), 1.0, 6.0, ((0, 32),))
    routes_keys = jax.random.split(jax.random.fold_in(key_list[2], 1), TOKENS // TOK_DEV)
    routes_turns = jax.random.permutation(jax.random.fold_in(key_list[2], 3), TOKENS // TOK_DEV)
    routes = jax.vmap(lambda own, number: deal_out(jax.random.fold_in(key_list[2], 2), own, number, TOK_DEV, EXPERTS, 2, CAP, 2))(routes_keys, routes_turns).reshape((TOKENS, 2))
    gates = jnp.clip(jnp.exp(math.log(1.0) - 1.609438 * jax.random.uniform(key_list[3], (TOKENS, 2), jnp.float32) ** block_scale(key_list[3], (TOKENS, 2), ((0, 32),), -0.2, 0.2)), 0.2, 1.0)
    w_gate = normal_values(key_list[4], (EXPERTS, D, FF), D ** -0.5, 0.109375, ((0, 2), (1, 16)))
    w_up = normal_values(key_list[5], (EXPERTS, D, FF), D ** -0.5, 0.109375, ((0, 2), (1, 16)))
    w_down_t = normal_values(key_list[6], (EXPERTS, D, FF), FF ** -0.5, 0.5, ((0, 2), (1, 16)))
    return {"tokens": tokens, "out_grad": out_grad, "routes": routes, "gates": gates, "w_gate": w_gate, "w_up": w_up, "w_down_t": w_down_t}


def reference(tokens, out_grad, routes, gates, w_gate, w_up, w_down_t):
    flat_routes = routes.reshape(-1)
    flat_gates = gates.reshape(-1)
    sorted_items = jnp.argsort(flat_routes, stable=True).astype(jnp.int32)
    row_limit = DEVICES * CAP
    padded = jnp.concatenate([sorted_items, jnp.zeros((row_limit,), jnp.int32)])
    token_grad = jnp.zeros(tokens.shape, jnp.float32)
    grads_in = []
    for expert in range(EXPERTS):
        first_row = jnp.sum(flat_routes < expert).astype(jnp.int32)
        live_count = jnp.sum(flat_routes == expert).astype(jnp.int32)
        picked = lax.dynamic_slice(padded, (first_row,), (row_limit,))
        live_rows = jnp.arange(row_limit, dtype=jnp.int32) < live_count
        token_index = (picked // 2).astype(jnp.int32)
        rows_in = tokens[token_index]
        slot_gates = jnp.where(live_rows, flat_gates[picked], 0.0)
        slot_grad = (out_grad[token_index].astype(jnp.float32) * slot_gates[:, None]).astype(jnp.bfloat16)
        in_weights = jnp.concatenate([w_gate[expert], w_up[expert]], axis=1)
        gate_up = jnp.dot(rows_in, in_weights, preferred_element_type=jnp.float32)
        gate_pre = gate_up[:, :FF]
        up_pre = gate_up[:, FF:]
        sigmoid_gate = jax.nn.sigmoid(gate_pre)
        silu_gate = gate_pre * sigmoid_gate
        act_grad = jnp.dot(slot_grad, w_down_t[expert], preferred_element_type=jnp.float32)
        gate_grad = act_grad * up_pre * sigmoid_gate * (1.0 + gate_pre * (1.0 - sigmoid_gate))
        up_grad = act_grad * silu_gate
        hidden_grad = jnp.concatenate([gate_grad, up_grad], axis=1).astype(jnp.bfloat16)
        slot_input = jnp.dot(hidden_grad, in_weights.T, preferred_element_type=jnp.float32).astype(jnp.bfloat16)
        token_grad = token_grad.at[token_index].add(jnp.where(live_rows[:, None], slot_input.astype(jnp.float32), 0.0))
        grads_in.append(jnp.dot(rows_in.T, hidden_grad, preferred_element_type=jnp.float32))
    grad_scale = 1.0 / math.sqrt(TOKENS)
    stacked_in = jnp.stack(grads_in) * grad_scale
    return (token_grad.astype(jnp.bfloat16), stacked_in[:, :, :FF], stacked_in[:, :, FF:])
```

```python
import functools
import math

import jax
import jax.numpy as jnp
from jax import lax
from jax.experimental import pallas as pl
from jax.experimental.pallas import tpu as pltpu
from jax.sharding import PartitionSpec as P

EXPERTS = 8
CAP = 40
INFO = 16
F32 = jnp.float32
BF16 = jnp.bfloat16


def remote(src, dst, send, recv, e, d):
    return pltpu.make_async_remote_copy(
        src_ref=src,
        dst_ref=dst,
        send_sem=send,
        recv_sem=recv,
        device_id={"expert": e, "dp": d},
        device_id_type=pl.DeviceIdType.MESH,
    )


def when(cond, fn):
    if cond is None:
        fn()
    else:
        pl.when(cond)(fn)


class Sends:
    def __init__(self):
        self.items = []

    def start(self, cond, make):
        when(cond, lambda: make().start())
        self.items.append((cond, make))

    def finish(self):
        for cond, make in self.items:
            when(cond, lambda make=make: make().wait_send())


def barrier(e, d, n_expert, n_data):
    sem = pltpu.get_barrier_semaphore()
    for j in range(1, n_data):
        pl.semaphore_signal(
            sem,
            inc=1,
            device_id={"expert": e, "dp": lax.rem(d + j, n_data)},
            device_id_type=pl.DeviceIdType.MESH,
        )
    for j in range(1, n_expert):
        pl.semaphore_signal(
            sem,
            inc=1,
            device_id={"expert": lax.rem(e + j, n_expert), "dp": d},
            device_id_type=pl.DeviceIdType.MESH,
        )
    pl.semaphore_wait(sem, n_data - 1 + n_expert - 1)


def both(p, q):
    if p is None:
        return q
    return jnp.logical_and(p, q)


def gather(e, d, n_data, owns, block, sems, sends, hook=None, use=None):
    up_s, down_s, b_s, c_s, recv = sems
    count = n_data // 4
    a, b, c = d // 4, lax.rem(d // 2, 2), lax.rem(d, 2)
    number = len(owns)

    def index(a2, b2, c2):
        return (a2 * 2 + b2) * 2 + c2

    def make(i, src, d2, target, send):
        return remote(src, block(i, d2), send, recv.at[i, d2], e, target)

    def arrive(i, d2):
        remote(block(i, d2), block(i, d2), c_s.at[i, 0], recv.at[i, d2], e, d).wait_recv()

    def pass_on(cond, i, src, a2, up, down, slot):
        d2 = index(a2, b, c)
        if up:
            sends.start(
                both(cond, a < count - 1),
                lambda: make(i, src(), d2, index(a + 1, b, c), up_s.at[i, slot]),
            )
        if down:
            sends.start(
                both(cond, a > 0),
                lambda: make(i, src(), d2, index(a - 1, b, c), down_s.at[i, slot]),
            )
        sends.start(cond, lambda: make(i, src(), d2, index(a, 1 - b, c), b_s.at[i, a2]))
        sends.start(cond, lambda: make(i, src(), d2, index(a, b, 1 - c), c_s.at[i, a2 * 2 + b]))

    def from_b(cond, a2):
        d2 = index(a2, 1 - b, c)
        for i in range(number):
            when(cond, lambda i=i: arrive(i, d2))
            sends.start(
                cond,
                lambda i=i: make(
                    i, block(i, d2), d2, index(a, b, 1 - c), c_s.at[i, a2 * 2 + 1 - b]
                ),
            )

    for step in range(count + 2):
        if step == 0:
            for i in range(number):
                pass_on(None, i, lambda i=i: owns[i], a, True, True, 0)
        elif step < count:
            for i in range(number):
                cond, a2 = a >= step, a - step
                d2 = index(a2, b, c)
                when(cond, lambda i=i, d2=d2: arrive(i, d2))
                pass_on(cond, i, lambda i=i, d2=d2: block(i, d2), a2, True, False, step)
                cond, a2 = a + step < count, a + step
                d2 = index(a2, b, c)
                when(cond, lambda i=i, d2=d2: arrive(i, d2))
                pass_on(cond, i, lambda i=i, d2=d2: block(i, d2), a2, False, True, step)
        if step == 1:
            from_b(None, a)
        elif 1 < step <= count:
            from_b(a >= step - 1, a - step + 1)
            from_b(a + step - 1 < count, a + step - 1)
        if hook is not None:
            hook(step, count)

        def job(j, carry, step=step):
            flip_b, flip_c, way = lax.rem(j // 2, 2), j // 4, lax.rem(j, 2)
            shift = step - flip_b - flip_c
            a2 = a - shift + 2 * shift * way
            d2 = index(a2, b + flip_b * (1 - 2 * b), c + flip_c * (1 - 2 * c))
            far = jnp.logical_or(shift > 0, jnp.logical_and(shift == 0, way == 0))
            valid = jnp.logical_and(far, jnp.logical_and(a2 >= 0, a2 < count))

            @pl.when(jnp.logical_and(valid, flip_c == 1))
            def _():
                for i in range(number):
                    arrive(i, d2)

            if use is not None:
                pl.when(valid)(lambda: use(d2))
            return carry

        lax.fori_loop(0, 8, job, 0)


def first_kernel(
    n_expert, n_data, w_g, w_u, w_dn, tok, og, info, blocks,
    all_g, all_u, all_dn, tx, ox, ix, tt,
    own_sem, up_s, down_s, b_s, c_s, recv, x_s, x_r, t_s, t_r, y_s, y_r,
):
    e, d = lax.axis_index("expert"), lax.axis_index("dp")
    width = w_g.shape[1]
    rows = tok.shape[0]

    def block(i, d2):
        return (all_g, all_u, all_dn)[i].at[:, pl.ds(d2 * width, width), :]

    def columns(e2, d2):
        return tt.at[:, pl.ds(pl.multiple_of((e2 * n_data + d2) * rows, rows), rows)]

    def half(e2):
        return tt.at[:, pl.ds(pl.multiple_of(e2 * n_data * rows, n_data * rows), n_data * rows)]

    own = [
        pltpu.make_async_copy(w_g, block(0, d), own_sem.at[0]),
        pltpu.make_async_copy(w_dn, block(2, d), own_sem.at[1]),
        pltpu.make_async_copy(tok, tx.at[e], own_sem.at[2]),
        pltpu.make_async_copy(og, ox.at[e], own_sem.at[3]),
        pltpu.make_async_copy(info, ix.at[e], own_sem.at[4]),
        pltpu.make_async_copy(blocks.at[d], columns(e, d), own_sem.at[5]),
        pltpu.make_async_copy(w_u, block(1, d), own_sem.at[6]),
    ]
    for copy in own:
        copy.start()
    barrier(e, d, n_expert, n_data)
    sends = Sends()
    triples = ((tok, tx), (og, ox), (info, ix))

    def hook(step, count):
        if step == 0:
            spread()
        if step == max(count - 2, 0):
            relay()

    def spread():
        for j in range(1, n_expert):
            for i, (src, dst) in enumerate(triples):
                sends.start(
                    None,
                    lambda i=i, j=j, src=src, dst=dst: remote(
                        src, dst.at[e], x_s.at[i, j], x_r.at[i, j], lax.rem(e + j, n_expert), d
                    ),
                )
        for j in range(1, n_data):
            sends.start(
                None,
                lambda j=j: remote(
                    blocks.at[lax.rem(d + j, n_data)], columns(e, d), t_s.at[j], t_r.at[j],
                    e, lax.rem(d + j, n_data),
                ),
            )

    def relay():
        own[5].wait()
        for j in range(1, n_data):
            source = lax.rem(d - j + n_data, n_data)
            place = columns(e, source)
            remote(place, place, t_s.at[j], t_r.at[j], e, source).wait_recv()
        for j in range(1, n_expert):
            sends.start(
                None,
                lambda j=j: remote(
                    half(e), half(e), y_s.at[j], y_r.at[j], lax.rem(e + j, n_expert), d
                ),
            )

    gather(e, d, n_data, (w_g, w_u, w_dn), block, (up_s, down_s, b_s, c_s, recv), sends, hook)
    for copy in own[:5] + own[6:]:
        copy.wait()
    for j in range(1, n_expert):
        source = lax.rem(e - j + n_expert, n_expert)
        for i, (src, dst) in enumerate(triples):
            remote(src, dst.at[source], x_s.at[i, j], x_r.at[i, j], source, d).wait_recv()
        remote(half(source), half(source), y_s.at[j], y_r.at[j], source, d).wait_recv()
    sends.finish()


def second_kernel(
    n_expert, n_data, scale, hid, ret, tt, tg, out_g, out_u,
    all_hid, rx, own_sem, up_s, down_s, b_s, c_s, recv, x_s, x_r,
):
    e, d = lax.axis_index("expert"), lax.axis_index("dp")
    local_count, width, hidden = out_g.shape
    rows = tt.shape[1] // (n_expert * n_data)

    def block(i, d2):
        return all_hid.at[d2]

    own = pltpu.make_async_copy(hid, block(0, d), own_sem)
    own.start()
    barrier(e, d, n_expert, n_data)
    sends = Sends()

    def hook(step, count):
        if step > 0:
            return
        for j in range(1, n_expert):
            target = lax.rem(e + j, n_expert)
            sends.start(
                None,
                lambda j=j, target=target: remote(
                    ret.at[target], rx.at[e], x_s.at[j], x_r.at[j], target, d
                ),
            )
        out_g[...] = jnp.zeros_like(out_g)
        out_u[...] = jnp.zeros_like(out_u)
        own.wait()

    def use(d2):
        parts = [
            tt[:, pl.ds(pl.multiple_of((s * n_data + d2) * rows, rows), rows)]
            for s in range(n_expert)
        ]
        both_tt = jnp.concatenate(parts, axis=1)
        tok, info = both_tt[:width], both_tt[width:].astype(F32)
        for x in range(local_count):
            expert = (e * local_count + x).astype(F32)
            pick = picker(info[0:1], info[1:2], info[2:3], info[3:4], expert, n_expert, rows)
            got = lax.dot_general(
                tok, pick, (((1,), (1,)), ((), ())), preferred_element_type=F32
            ).astype(BF16)
            term = jnp.dot(got, all_hid[d2, x], preferred_element_type=F32)
            out_g[x] += term[:, :hidden]
            out_u[x] += term[:, hidden:]

    gather(e, d, n_data, (hid,), block, (up_s, down_s, b_s, c_s, recv), sends, hook, use)
    out_g[...] = out_g[...] * scale
    out_u[...] = out_u[...] * scale
    total = ret[e].astype(F32)
    for j in range(1, n_expert):
        source = lax.rem(e - j + n_expert, n_expert)
        remote(ret.at[source], rx.at[source], x_s.at[j], x_r.at[j], source, d).wait_recv()
        total += rx[source].astype(F32)
    tg[...] = total.astype(BF16)
    sends.finish()


def picker(e0, p0, e1, p1, expert, n_expert, rows):
    shape = (n_expert * CAP, n_expert * rows)
    slot = lax.broadcasted_iota(jnp.int32, shape, 0)
    base = (lax.broadcasted_iota(jnp.int32, (1, shape[1]), 1) // rows) * CAP
    want0 = jnp.where(e0 == expert, p0.astype(jnp.int32) + base, -1)
    want1 = jnp.where(e1 == expert, p1.astype(jnp.int32) + base, -1)
    hit = jnp.logical_or(slot == want0, slot == want1)
    return jnp.where(hit, 1.0, 0.0).astype(BF16)


def compute_kernel(n_expert, tx, ox, ix, w_g, w_u, w_dn, hid, ret, acc):
    x, local_count = pl.program_id(0), pl.num_programs(0)
    hidden = w_dn.shape[2]
    rows = tx.shape[0] // n_expert
    expert = (lax.axis_index("expert") * local_count + x).astype(F32)
    info_r = jnp.concatenate([ix[s] for s in range(n_expert)], axis=1)
    info_c = info_r.T
    w_in = jnp.concatenate([w_g[0], w_u[0]], axis=1)
    gate_up = jnp.dot(tx[...], w_in, preferred_element_type=F32)
    back = jnp.dot(ox[...], w_dn[0], preferred_element_type=F32)
    gate = jnp.where(info_c[:, 0:1] == expert, info_c[:, 4:5], 0.0) + jnp.where(
        info_c[:, 2:3] == expert, info_c[:, 5:6], 0.0
    )
    act_grad = back * gate
    gate_pre, up_pre = gate_up[:, :hidden], gate_up[:, hidden:]
    s = jax.nn.sigmoid(gate_pre)
    gate_grad = act_grad * up_pre * s * (1.0 + gate_pre * (1.0 - s))
    up_grad = act_grad * (gate_pre * s)
    grad = jnp.concatenate([gate_grad, up_grad], axis=1).astype(BF16)
    pick = picker(
        info_r[0:1, :], info_r[1:2, :], info_r[2:3, :], info_r[3:4, :], expert, n_expert, rows
    )
    hid[0] = jnp.dot(pick, grad, preferred_element_type=F32).astype(BF16)
    term = lax.dot_general(grad, w_in, (((1,), (1,)), ((), ())), preferred_element_type=F32)

    @pl.when(x == 0)
    def _():
        acc[...] = term

    @pl.when(x > 0)
    def _():
        acc[...] += term

    @pl.when(x == local_count - 1)
    def _():
        ret[...] = acc[...].astype(BF16)


def local(tokens, out_grad, routes, gates, w_gate, w_up, w_down_t):
    rows, model = tokens.shape
    n_expert = lax.axis_size("expert")
    n_data = lax.axis_size("dp")
    local_count, width, hidden = w_gate.shape
    count = n_data // 4
    any_, vmem = pl.BlockSpec(memory_space=pl.ANY), pl.BlockSpec(memory_space=pltpu.VMEM)
    dma = pltpu.SemaphoreType.DMA

    flat = routes.reshape(-1)
    item = jnp.arange(flat.shape[0], dtype=jnp.int32)
    earlier = jnp.logical_and(flat[:, None] == flat[None, :], item[None, :] < item[:, None])
    position = jnp.sum(earlier.astype(jnp.int32), axis=1).reshape(rows, 2)
    info = jnp.stack(
        [
            routes[:, 0].astype(F32), position[:, 0].astype(F32),
            routes[:, 1].astype(F32), position[:, 1].astype(F32),
            gates[:, 0], gates[:, 1], gates[:, 0], gates[:, 1],
        ]
    )
    side = jnp.concatenate([info[:4].astype(BF16), jnp.zeros((INFO - 4, rows), BF16)], axis=0)
    blocks = jnp.concatenate(
        [
            tokens.T.reshape(n_data, width, rows),
            jnp.broadcast_to(side[None], (n_data, INFO, rows)),
        ],
        axis=1,
    )

    def chain_sems(number):
        return [
            dma((number, count)), dma((number, count)), dma((number, count)),
            dma((number, 2 * count)), dma((number, n_data)),
        ]

    shape = jax.ShapeDtypeStruct
    all_g, all_u, all_dn, tx, ox, ix, tt = pl.pallas_call(
        functools.partial(first_kernel, n_expert, n_data),
        out_shape=(
            shape((local_count, model, hidden), BF16),
            shape((local_count, model, hidden), BF16),
            shape((local_count, model, hidden), BF16),
            shape((n_expert, rows, model), BF16),
            shape((n_expert, rows, model), BF16),
            shape((n_expert, 8, rows), F32),
            shape((width + INFO, n_expert * n_data * rows), BF16),
        ),
        in_specs=[vmem] * 7,
        out_specs=[any_] * 7,
        scratch_shapes=[dma((7,))]
        + chain_sems(3)
        + [
            dma((3, n_expert)), dma((3, n_expert)), dma((n_data,)), dma((n_data,)),
            dma((n_expert,)), dma((n_expert,)),
        ],
        compiler_params=pltpu.CompilerParams(collective_id=0, has_side_effects=True),
    )(w_gate, w_up, w_down_t, tokens, out_grad, info, blocks)

    total = n_expert * rows
    slots = n_expert * CAP
    hid, ret = pl.pallas_call(
        functools.partial(compute_kernel, n_expert),
        grid=(local_count,),
        out_shape=(shape((local_count, slots, 2 * hidden), BF16), shape((total, model), BF16)),
        in_specs=[
            pl.BlockSpec((total, model), lambda x: (0, 0)),
            pl.BlockSpec((total, model), lambda x: (0, 0)),
            pl.BlockSpec((n_expert, 8, rows), lambda x: (0, 0, 0)),
            pl.BlockSpec((1, model, hidden), lambda x: (x, 0, 0)),
            pl.BlockSpec((1, model, hidden), lambda x: (x, 0, 0)),
            pl.BlockSpec((1, model, hidden), lambda x: (x, 0, 0)),
        ],
        out_specs=[
            pl.BlockSpec((1, slots, 2 * hidden), lambda x: (x, 0, 0)),
            pl.BlockSpec((total, model), lambda x: (0, 0)),
        ],
        scratch_shapes=[pltpu.VMEM((total, model), F32)],
        compiler_params=pltpu.CompilerParams(vmem_limit_bytes=60 * 1024 * 1024),
    )(tx.reshape(total, model), ox.reshape(total, model), ix, all_g, all_u, all_dn)

    grad_scale = 1.0 / math.sqrt(rows * n_expert * n_data)
    token_grad, grad_gate, grad_up = pl.pallas_call(
        functools.partial(second_kernel, n_expert, n_data, grad_scale),
        out_shape=(
            shape((rows, model), BF16),
            shape((local_count, width, hidden), F32),
            shape((local_count, width, hidden), F32),
        ),
        in_specs=[vmem] * 3,
        out_specs=[vmem] * 3,
        scratch_shapes=[
            pltpu.VMEM((n_data, local_count, slots, 2 * hidden), BF16),
            pltpu.VMEM((n_expert, rows, model), BF16),
            dma,
        ]
        + chain_sems(1)
        + [dma((n_expert,)), dma((n_expert,))],
        compiler_params=pltpu.CompilerParams(
            collective_id=1, has_side_effects=True, vmem_limit_bytes=60 * 1024 * 1024
        ),
    )(hid, ret.reshape(n_expert, rows, model), tt)
    return token_grad, grad_gate, grad_up


def solution(mesh):
    row, split = P(("expert", "dp"), None), P("expert", "dp", None)
    return jax.shard_map(
        local,
        mesh=mesh,
        in_specs=(row, row, row, row, split, split, split),
        out_specs=(row, split, split),
        check_vma=False,
    )
```

```python
import functools
import math

import jax
import jax.numpy as jnp
from jax import lax
from jax.experimental import pallas as pl
from jax.experimental.pallas import tpu as pltpu
from jax.sharding import PartitionSpec as P

EXPERTS = 8
CAP = 40
INFO = 16
F32 = jnp.float32
BF16 = jnp.bfloat16


def remote(src, dst, send, recv, e, d):
    return pltpu.make_async_remote_copy(
        src_ref=src,
        dst_ref=dst,
        send_sem=send,
        recv_sem=recv,
        device_id={"expert": e, "dp": d},
        device_id_type=pl.DeviceIdType.MESH,
    )


def when(cond, fn):
    if cond is None:
        fn()
    else:
        pl.when(cond)(fn)


class Sends:
    def __init__(self):
        self.items = []

    def start(self, cond, make):
        when(cond, lambda: make().start())
        self.items.append((cond, make))

    def finish(self):
        for cond, make in self.items:
            when(cond, lambda make=make: make().wait_send())


def barrier(e, d, n_expert, n_data):
    sem = pltpu.get_barrier_semaphore()
    for j in range(1, n_data):
        pl.semaphore_signal(
            sem,
            inc=1,
            device_id={"expert": e, "dp": lax.rem(d + j, n_data)},
            device_id_type=pl.DeviceIdType.MESH,
        )
    for j in range(1, n_expert):
        pl.semaphore_signal(
            sem,
            inc=1,
            device_id={"expert": lax.rem(e + j, n_expert), "dp": d},
            device_id_type=pl.DeviceIdType.MESH,
        )
    pl.semaphore_wait(sem, n_data - 1 + n_expert - 1)


def both(p, q):
    if p is None:
        return q
    return jnp.logical_and(p, q)


class Chain:
    def __init__(self, e, d, n_data, block, sems, sends):
        self.e, self.block, self.sems, self.sends = e, block, sems, sends
        self.count = n_data // 4
        self.abc = d // 4, lax.rem(d // 2, 2), lax.rem(d, 2)

    def index(self, a, b, c):
        return (a * 2 + b) * 2 + c

    def arrive(self, i, d2):
        block = self.block(i, d2)
        up_s, down_s, b_s, c_s, recv = self.sems
        remote(block, block, c_s.at[i, 0], recv.at[i, d2], self.e, self.index(*self.abc)).wait_recv()

    def send(self, cond, i, d2, target, sem):
        recv = self.sems[4]
        self.sends.start(
            cond,
            lambda: remote(self.block(i, d2), self.block(i, d2), sem, recv.at[i, d2], self.e, target),
        )

    def pass_on(self, cond, i, a2, up, down, slot):
        (a, b, c), index, count = self.abc, self.index, self.count
        up_s, down_s, b_s, c_s, _ = self.sems
        d2 = index(a2, b, c)
        self.send(cond, i, d2, index(a, 1 - b, c), b_s.at[i, a2])
        if up:
            self.send(both(cond, a < count - 1), i, d2, index(a + 1, b, c), up_s.at[i, slot])
        if down:
            self.send(both(cond, a > 0), i, d2, index(a - 1, b, c), down_s.at[i, slot])
        self.send(cond, i, d2, index(a, b, 1 - c), c_s.at[i, a2 * 2 + b])

    def from_b(self, cond, i, a2):
        a, b, c = self.abc
        d2 = self.index(a2, 1 - b, c)
        when(cond, lambda: self.arrive(i, d2))
        self.send(cond, i, d2, self.index(a, b, 1 - c), self.sems[3].at[i, a2 * 2 + 1 - b])

    def step(self, i, s):
        (a, b, c), count = self.abc, self.count
        if s == 0:
            self.pass_on(None, i, a, True, True, 0)
        elif s < count:
            for cond, a2, up in ((a >= s, a - s, True), (a + s < count, a + s, False)):
                d2 = self.index(a2, b, c)
                when(cond, lambda d2=d2: self.arrive(i, d2))
                self.pass_on(cond, i, a2, up, not up, s)
        if s == 1:
            self.from_b(None, i, a)
        elif 1 < s <= count:
            self.from_b(a >= s - 1, i, a - s + 1)
            self.from_b(a + s - 1 < count, i, a + s - 1)

    def finish(self, i):
        c = self.abc[2]

        def one(j, carry):
            self.arrive(i, 2 * j + 1 - c)
            return carry

        lax.fori_loop(0, 2 * self.count, one, 0)


def fused_kernel(
    n_expert, n_data, scale, tok, og, routes, gates, w_g, w_u, w_dn,
    tg, out_g, out_u,
    w_all, tx, ox, ix, blocks, tt, slots, acc, hid, ret, rx,
    own_sem, up_s, down_s, b_s, c_s, w_recv, hup_s, hdown_s, hb_s, hc_s, h_recv,
    x_s, x_r, t_s, t_r, y_s, y_r, r_s, r_r,
):
    e, d = lax.axis_index("expert"), lax.axis_index("dp")
    local_count, width, hidden = out_g.shape
    rows, model = tg.shape
    span = slots.shape[2] // n_data
    used = n_expert * CAP
    chunks, chunk = ret.shape[0], ret.shape[3]
    last = local_count - 1

    def w_block(i, d2):
        return w_all.at[i, pl.ds(d2 * width, width), :]

    groups = [(0, last), (last, local_count)] if last else [(0, 1)]

    def h_block(i, d2):
        low, high = groups[i]
        return hid.at[pl.ds(low, high - low), d2, pl.ds(0, used), :]

    def mine(ref, e2):
        return ref.at[pl.ds(e2 * rows, rows), :]

    own = [
        pltpu.make_async_copy(
            w, w_all.at[:, pl.ds(d * width, width), pl.ds(i * hidden, hidden)], own_sem.at[i]
        )
        for i, w in enumerate((w_g, w_u, w_dn))
    ] + [
        pltpu.make_async_copy(tok, mine(tx, e), own_sem.at[3]),
        pltpu.make_async_copy(og, mine(ox, e), own_sem.at[4]),
    ]
    for copy in own:
        copy.start()
    barrier(e, d, n_expert, n_data)
    sends = Sends()
    weights = Chain(e, d, n_data, w_block, (up_s, down_s, b_s, c_s, w_recv), sends)
    grads = Chain(e, d, n_data, h_block, (hup_s, hdown_s, hb_s, hc_s, h_recv), sends)

    for copy in own[:3]:
        copy.wait()
    weights.step(0, 0)
    pairs = ((tok, tx, 0), (og, ox, 1))
    for j in range(1, n_expert):
        for src, dst, i in pairs:
            sends.start(
                None,
                lambda src=src, dst=dst, i=i, j=j: remote(
                    src, mine(dst, e), x_s.at[i, j], x_r.at[i, j], lax.rem(e + j, n_expert), d
                ),
            )

    def prepare():
        e0, e1 = routes[0:1, :].astype(F32), routes[1:2, :].astype(F32)
        name = lax.broadcasted_iota(jnp.int32, (EXPERTS, rows), 0).astype(F32)
        hot0, hot1 = jnp.where(e0 == name, 1.0, 0.0), jnp.where(e1 == name, 1.0, 0.0)
        before = jnp.where(
            lax.broadcasted_iota(jnp.int32, (rows, rows), 0)
            < lax.broadcasted_iota(jnp.int32, (rows, rows), 1),
            1.0, 0.0,
        ).astype(BF16)
        seen = jnp.dot((hot0 + hot1).astype(BF16), before, preferred_element_type=F32)
        p0 = jnp.sum(seen * hot0, axis=0, keepdims=True)
        p1 = jnp.sum(seen * hot1, axis=0, keepdims=True)
        g = gates[...]
        info = jnp.concatenate([e0, p0, e1, p1, g, g], axis=0)
        ix[e] = info
        for j in range(1, n_expert):
            sends.start(
                None,
                lambda j=j: remote(
                    ix.at[e], ix.at[e], x_s.at[2, j], x_r.at[2, j], lax.rem(e + j, n_expert), d
                ),
            )
        side = jnp.concatenate([info, jnp.zeros_like(info)], axis=0).astype(BF16)
        own[3].wait()
        piece = 384
        for j in range(model // piece):
            part = tx[pl.ds(pl.multiple_of(e * rows, rows), rows), j * piece : (j + 1) * piece].T
            for k in range(piece // width):
                blocks[j * (piece // width) + k, :width, :] = part[k * width : (k + 1) * width]
        for j in range(n_data):
            blocks[j, width:, :] = side
        tt[e, d] = blocks[d]
        hid[:, :, used:, :] = jnp.zeros((local_count, n_data, span - used, 2 * hidden), BF16)

    def spread():
        for j in range(1, n_data):
            sends.start(
                None,
                lambda j=j: remote(
                    blocks.at[lax.rem(d + j, n_data)], tt.at[e, d], t_s.at[j], t_r.at[j],
                    e, lax.rem(d + j, n_data),
                ),
            )

    def relay():
        for j in range(1, n_data):
            source = lax.rem(d - j + n_data, n_data)
            place = tt.at[e, source]
            remote(place, place, t_s.at[j], t_r.at[j], e, source).wait_recv()
        for j in range(1, n_expert):
            sends.start(
                None,
                lambda j=j: remote(
                    tt.at[e], tt.at[e], y_s.at[j], y_r.at[j], lax.rem(e + j, n_expert), d
                ),
            )

    def partners():
        own[4].wait()
        for j in range(1, n_expert):
            source = lax.rem(e - j + n_expert, n_expert)
            for src, dst, i in pairs:
                remote(src, mine(dst, source), x_s.at[i, j], x_r.at[i, j], source, d).wait_recv()
            remote(ix.at[e], ix.at[source], x_s.at[2, j], x_r.at[2, j], source, d).wait_recv()

    def compute(x):
        weights.finish(x)
        expert = (e * local_count + x).astype(F32)
        info_r = jnp.concatenate([ix[s] for s in range(n_expert)], axis=1)
        info_c = info_r.T
        gate_up = jnp.dot(tx[...], w_all[x, :, : 2 * hidden], preferred_element_type=F32)
        back = jnp.dot(ox[...], w_all[x, :, 2 * hidden :], preferred_element_type=F32)
        gate = jnp.where(info_c[:, 0:1] == expert, info_c[:, 4:5], 0.0) + jnp.where(
            info_c[:, 2:3] == expert, info_c[:, 5:6], 0.0
        )
        act_grad = back * gate
        gate_pre, up_pre = gate_up[:, :hidden], gate_up[:, hidden:]
        s = jax.nn.sigmoid(gate_pre)
        gate_grad = act_grad * up_pre * s * (1.0 + gate_pre * (1.0 - s))
        up_grad = act_grad * (gate_pre * s)
        grad = jnp.concatenate([gate_grad, up_grad], axis=1).astype(BF16)
        pick = picker(
            info_r[0:1, :], info_r[1:2, :], info_r[2:3, :], info_r[3:4, :], expert, n_expert, rows
        )
        hid[x, d, :used, :] = jnp.dot(pick, grad, preferred_element_type=F32).astype(BF16)
        if x == last:
            grads.step(len(groups) - 1, 0)
        for k in range(chunks):
            place = slice(k * chunk, (k + 1) * chunk)
            term = lax.dot_general(
                grad, w_all[x, place, : 2 * hidden], (((1,), (1,)), ((), ())),
                preferred_element_type=F32,
            )
            if x > 0:
                term += acc[:, place]
            if x < last:
                acc[:, place] = term
                continue
            for s2 in range(n_expert):
                ret[k, s2] = term[s2 * rows : (s2 + 1) * rows].astype(BF16)
            for j in range(1, n_expert):
                target = lax.rem(e + j, n_expert)
                sends.start(
                    None,
                    lambda k=k, j=j, target=target: remote(
                        ret.at[k, target], rx.at[k, e], r_s.at[k, j], r_r.at[k, j], target, d
                    ),
                )

    count = n_data // 4
    places = [(last - 1, count)] + [(last, s) for s in range(1, count + 1)]
    hooks = {place: [functools.partial(compute, x)] for x, place in zip(range(last), places)}
    if last:
        hooks[places[0]].insert(0, partners)
    hooks.setdefault((0, count), []).insert(0, spread)
    hooks.setdefault((min(1, last), count), []).insert(1 if last == 0 else 0, relay)
    prepare()
    for x in range(local_count):
        for s in range(1, count + 1):
            if s == count and x < last:
                weights.step(x + 1, 0)
            weights.step(x, s)
            for job in hooks.get((x, s), []):
                job()
    if last:
        grads.step(0, 0)
    else:
        partners()
    compute(last)

    for j in range(1, n_expert):
        source = lax.rem(e - j + n_expert, n_expert)
        remote(tt.at[source], tt.at[source], y_s.at[j], y_r.at[j], source, d).wait_recv()
    row = lax.broadcasted_iota(jnp.int32, (local_count * span, n_expert * rows), 0)
    base = (lax.broadcasted_iota(jnp.int32, (1, n_expert * rows), 1) // rows) * CAP

    def reorder(d2, carry):
        joined = jnp.concatenate([tt[s, d2] for s in range(n_expert)], axis=1)
        info = joined[width:].astype(F32).astype(jnp.int32)
        place0 = (info[0:1] - e * local_count) * span + info[1:2] + base
        place1 = (info[2:3] - e * local_count) * span + info[3:4] + base
        hit = jnp.logical_or(row == place0, row == place1)
        pick = jnp.where(hit, 1.0, 0.0).astype(BF16)
        got = lax.dot_general(
            joined[:width], pick, (((1,), (1,)), ((), ())), preferred_element_type=F32
        ).astype(BF16)
        for x in range(local_count):
            slots[x, :, pl.ds(pl.multiple_of(d2 * span, span), span)] = got[
                :, x * span : (x + 1) * span
            ]
        return carry

    done = 0
    for s in range(1, count + 1):
        for i in range(len(groups)):
            grads.step(i, s)
        until = n_data * s // count
        lax.fori_loop(done, until, reorder, 0)
        done = until
    for i, (low, high) in enumerate(groups):
        grads.finish(i)
        for x in range(low, high):
            flat = hid[x].reshape(n_data * span, 2 * hidden)
            term = jnp.dot(slots[x], flat, preferred_element_type=F32) * scale
            out_g[x] = term[:, :hidden]
            out_u[x] = term[:, hidden:]
    for k in range(chunks):
        total = ret[k, e].astype(F32)
        for j in range(1, n_expert):
            source = lax.rem(e - j + n_expert, n_expert)
            remote(ret.at[k, e], rx.at[k, source], r_s.at[k, j], r_r.at[k, j], source, d).wait_recv()
            total += rx[k, source].astype(F32)
        tg[:, k * chunk : (k + 1) * chunk] = total.astype(BF16)
    sends.finish()


def picker(e0, p0, e1, p1, expert, n_expert, rows):
    shape = (n_expert * CAP, n_expert * rows)
    slot = lax.broadcasted_iota(jnp.int32, shape, 0)
    base = (lax.broadcasted_iota(jnp.int32, (1, shape[1]), 1) // rows) * CAP
    want0 = jnp.where(e0 == expert, p0.astype(jnp.int32) + base, -1)
    want1 = jnp.where(e1 == expert, p1.astype(jnp.int32) + base, -1)
    hit = jnp.logical_or(slot == want0, slot == want1)
    return jnp.where(hit, 1.0, 0.0).astype(BF16)


def local(tokens, out_grad, routes, gates, w_gate, w_up, w_down_t):
    rows, model = tokens.shape
    n_expert = lax.axis_size("expert")
    n_data = lax.axis_size("dp")
    local_count, width, hidden = w_gate.shape
    count = n_data // 4
    any_, vmem = pl.BlockSpec(memory_space=pl.ANY), pl.BlockSpec(memory_space=pltpu.VMEM)
    dma = pltpu.SemaphoreType.DMA
    total, span = n_expert * rows, -(-n_expert * CAP // 128) * 128
    chunks = 4

    def chain_sems(number):
        return [
            dma((number, count)), dma((number, count)), dma((number, count)),
            dma((number, 2 * count)), dma((number, n_data)),
        ]

    shape = jax.ShapeDtypeStruct
    return pl.pallas_call(
        functools.partial(
            fused_kernel, n_expert, n_data, 1.0 / math.sqrt(rows * n_expert * n_data)
        ),
        out_shape=(
            shape((rows, model), BF16),
            shape((local_count, width, hidden), F32),
            shape((local_count, width, hidden), F32),
        ),
        in_specs=[any_, any_, vmem, vmem, any_, any_, any_],
        out_specs=[vmem] * 3,
        scratch_shapes=[
            pltpu.VMEM((local_count, model, 3 * hidden), BF16),
            pltpu.VMEM((total, model), BF16),
            pltpu.VMEM((total, model), BF16),
            pltpu.VMEM((n_expert, 8, rows), F32),
            pltpu.VMEM((n_data, width + INFO, rows), BF16),
            pltpu.VMEM((n_expert, n_data, width + INFO, rows), BF16),
            pltpu.VMEM((local_count, width, n_data * span), BF16),
            pltpu.VMEM((total, model) if local_count > 1 else (8, 128), F32),
            pltpu.VMEM((local_count, n_data, span, 2 * hidden), BF16),
            pltpu.VMEM((chunks, n_expert, rows, model // chunks), BF16),
            pltpu.VMEM((chunks, n_expert, rows, model // chunks), BF16),
            dma((5,)),
        ]
        + chain_sems(local_count)
        + chain_sems(min(2, local_count))
        + [
            dma((3, n_expert)), dma((3, n_expert)), dma((n_data,)), dma((n_data,)),
            dma((n_expert,)), dma((n_expert,)), dma((chunks, n_expert)), dma((chunks, n_expert)),
        ],
        compiler_params=pltpu.CompilerParams(
            collective_id=0, has_side_effects=True, vmem_limit_bytes=60 * 1024 * 1024
        ),
    )(tokens, out_grad, routes.T, gates.T, w_gate, w_up, w_down_t)


def solution(mesh):
    row, split = P(("expert", "dp"), None), P("expert", "dp", None)
    return jax.shard_map(
        local,
        mesh=mesh,
        in_specs=(row, row, row, row, split, split, split),
        out_specs=(row, split, split),
        check_vma=False,
    )
```

```python
import functools
import math

import jax
import jax.numpy as jnp
from jax import lax
from jax.experimental import pallas as pl
from jax.experimental.pallas import tpu as pltpu
from jax.sharding import PartitionSpec as P

EXPERTS = 8
CAP = 40
INFO = 16
F32 = jnp.float32
BF16 = jnp.bfloat16


def remote(src, dst, send, recv, e, d):
    return pltpu.make_async_remote_copy(
        src_ref=src,
        dst_ref=dst,
        send_sem=send,
        recv_sem=recv,
        device_id={"expert": e, "dp": d},
        device_id_type=pl.DeviceIdType.MESH,
    )


def when(cond, fn):
    if cond is None:
        fn()
    else:
        pl.when(cond)(fn)


class Sends:
    def __init__(self):
        self.items = []

    def start(self, cond, make):
        when(cond, lambda: make().start())
        self.items.append((cond, make))

    def finish(self):
        for cond, make in self.items:
            when(cond, lambda make=make: make().wait_send())


def barrier(e, d, n_expert, n_data):
    sem = pltpu.get_barrier_semaphore()
    for j in range(1, n_data):
        pl.semaphore_signal(
            sem,
            inc=1,
            device_id={"expert": e, "dp": lax.rem(d + j, n_data)},
            device_id_type=pl.DeviceIdType.MESH,
        )
    for j in range(1, n_expert):
        pl.semaphore_signal(
            sem,
            inc=1,
            device_id={"expert": lax.rem(e + j, n_expert), "dp": d},
            device_id_type=pl.DeviceIdType.MESH,
        )
    pl.semaphore_wait(sem, n_data - 1 + n_expert - 1)


def both(p, q):
    if p is None:
        return q
    return jnp.logical_and(p, q)


class Chain:
    def __init__(self, e, d, n_data, block, sems, sends):
        self.e, self.block, self.sems, self.sends = e, block, sems, sends
        self.count = n_data // 4
        self.abc = d // 4, lax.rem(d // 2, 2), lax.rem(d, 2)

    def index(self, a, b, c):
        return (a * 2 + b) * 2 + c

    def arrive(self, i, d2):
        block = self.block(i, d2)
        up_s, down_s, b_s, c_s, recv = self.sems
        remote(block, block, c_s.at[i, 0], recv.at[i, d2], self.e, self.index(*self.abc)).wait_recv()

    def send(self, cond, i, d2, target, sem):
        recv = self.sems[4]
        self.sends.start(
            cond,
            lambda: remote(self.block(i, d2), self.block(i, d2), sem, recv.at[i, d2], self.e, target),
        )

    def pass_on(self, cond, i, a2, up, down, slot):
        (a, b, c), index, count = self.abc, self.index, self.count
        up_s, down_s, b_s, c_s, _ = self.sems
        d2 = index(a2, b, c)
        self.send(cond, i, d2, index(a, 1 - b, c), b_s.at[i, a2])
        if up:
            self.send(both(cond, a < count - 1), i, d2, index(a + 1, b, c), up_s.at[i, slot])
        if down:
            self.send(both(cond, a > 0), i, d2, index(a - 1, b, c), down_s.at[i, slot])
        self.send(cond, i, d2, index(a, b, 1 - c), c_s.at[i, a2 * 2 + b])

    def from_b(self, cond, i, a2):
        a, b, c = self.abc
        d2 = self.index(a2, 1 - b, c)
        when(cond, lambda: self.arrive(i, d2))
        self.send(cond, i, d2, self.index(a, b, 1 - c), self.sems[3].at[i, a2 * 2 + 1 - b])

    def step(self, i, s):
        (a, b, c), count = self.abc, self.count
        if s == 0:
            self.pass_on(None, i, a, True, True, 0)
        elif s < count:
            for cond, a2, up in ((a >= s, a - s, True), (a + s < count, a + s, False)):
                d2 = self.index(a2, b, c)
                when(cond, lambda d2=d2: self.arrive(i, d2))
                self.pass_on(cond, i, a2, up, not up, s)

    def step_b(self, i, s):
        a, count = self.abc[0], self.count
        if s == 1:
            self.from_b(None, i, a)
        else:
            self.from_b(a >= s - 1, i, a - s + 1)
            self.from_b(a + s - 1 < count, i, a + s - 1)

    def finish(self, i):
        c = self.abc[2]

        def one(j, carry):
            self.arrive(i, 2 * j + 1 - c)
            return carry

        lax.fori_loop(0, 2 * self.count, one, 0)


def fused_kernel(
    n_expert, n_data, scale, tok, og, routes, gates, w_g, w_u, w_dn,
    tg, out_g, out_u,
    w_all, tx, ox, ix, blocks, tt, slots, acc, hid, grad_s, ret, rx,
    own_sem, up_s, down_s, b_s, c_s, w_recv, hup_s, hdown_s, hb_s, hc_s, h_recv,
    x_s, x_r, t_s, t_r, y_s, y_r, r_s, r_r,
):
    e, d = lax.axis_index("expert"), lax.axis_index("dp")
    local_count, width, hidden = out_g.shape
    rows, model = tg.shape
    span = slots.shape[2] // n_data
    used = n_expert * CAP
    half = model // 2
    last = local_count - 1

    def w_block(i, d2):
        return w_all.at[i, pl.ds(d2 * width, width), :]

    groups = [(0, last), (last, local_count)] if last else [(0, 1)]

    def h_block(i, d2):
        low, high = groups[i]
        return hid.at[pl.ds(low, high - low), d2, pl.ds(0, used), :]

    def mine(ref, e2):
        return ref.at[pl.ds(e2 * rows, rows), :]

    own = [
        pltpu.make_async_copy(
            w, w_all.at[:, pl.ds(d * width, width), pl.ds(i * hidden, hidden)], own_sem.at[i]
        )
        for i, w in enumerate((w_g, w_u, w_dn))
    ] + [
        pltpu.make_async_copy(tok, mine(tx, e), own_sem.at[3]),
        pltpu.make_async_copy(og, mine(ox, e), own_sem.at[4]),
    ]
    for copy in own:
        copy.start()
    barrier(e, d, n_expert, n_data)
    sends = Sends()
    weights = Chain(e, d, n_data, w_block, (up_s, down_s, b_s, c_s, w_recv), sends)
    grads = Chain(e, d, n_data, h_block, (hup_s, hdown_s, hb_s, hc_s, h_recv), sends)

    for copy in own[:3]:
        copy.wait()
    weights.step(0, 0)
    pairs = ((tok, tx, 0), (og, ox, 1))
    for j in range(1, n_expert):
        for src, dst, i in pairs:
            sends.start(
                None,
                lambda src=src, dst=dst, i=i, j=j: remote(
                    src, mine(dst, e), x_s.at[i, j], x_r.at[i, j], lax.rem(e + j, n_expert), d
                ),
            )

    def prepare():
        e0, e1 = routes[0:1, :].astype(F32), routes[1:2, :].astype(F32)
        name = lax.broadcasted_iota(jnp.int32, (EXPERTS, rows), 0).astype(F32)
        hot0, hot1 = jnp.where(e0 == name, 1.0, 0.0), jnp.where(e1 == name, 1.0, 0.0)
        before = jnp.where(
            lax.broadcasted_iota(jnp.int32, (rows, rows), 0)
            < lax.broadcasted_iota(jnp.int32, (rows, rows), 1),
            1.0, 0.0,
        ).astype(BF16)
        seen = jnp.dot((hot0 + hot1).astype(BF16), before, preferred_element_type=F32)
        p0 = jnp.sum(seen * hot0, axis=0, keepdims=True)
        p1 = jnp.sum(seen * hot1, axis=0, keepdims=True)
        g = gates[...]
        info = jnp.concatenate([e0, p0, e1, p1, g, g], axis=0)
        ix[e] = info
        for j in range(1, n_expert):
            sends.start(
                None,
                lambda j=j: remote(
                    ix.at[e], ix.at[e], x_s.at[2, j], x_r.at[2, j], lax.rem(e + j, n_expert), d
                ),
            )
        side = jnp.concatenate([info, jnp.zeros_like(info)], axis=0).astype(BF16)
        own[3].wait()
        piece = 384
        for j in range(model // piece):
            part = tx[pl.ds(pl.multiple_of(e * rows, rows), rows), j * piece : (j + 1) * piece].T
            for k in range(piece // width):
                blocks[j * (piece // width) + k, :width, :] = part[k * width : (k + 1) * width]
        for j in range(n_data):
            blocks[j, width:, :] = side
        tt[e, d] = blocks[d]
        hid[:, :, used:, :] = jnp.zeros((local_count, n_data, span - used, 2 * hidden), BF16)

    def spread():
        for j in range(1, n_data):
            sends.start(
                None,
                lambda j=j: remote(
                    blocks.at[lax.rem(d + j, n_data)], tt.at[e, d], t_s.at[j], t_r.at[j],
                    e, lax.rem(d + j, n_data),
                ),
            )

    def relay():
        for j in range(1, n_data):
            source = lax.rem(d - j + n_data, n_data)
            place = tt.at[e, source]
            remote(place, place, t_s.at[j], t_r.at[j], e, source).wait_recv()
        for j in range(1, n_expert):
            sends.start(
                None,
                lambda j=j: remote(
                    tt.at[e], tt.at[e], y_s.at[j], y_r.at[j], lax.rem(e + j, n_expert), d
                ),
            )
        lax.fori_loop(0, n_data, functools.partial(reorder, e, True), 0)

    def partners():
        own[4].wait()
        for j in range(1, n_expert):
            source = lax.rem(e - j + n_expert, n_expert)
            for src, dst, i in pairs:
                remote(src, mine(dst, source), x_s.at[i, j], x_r.at[i, j], source, d).wait_recv()
            remote(ix.at[e], ix.at[source], x_s.at[2, j], x_r.at[2, j], source, d).wait_recv()

    def compute(x):
        weights.finish(x)
        expert = (e * local_count + x).astype(F32)
        info_r = jnp.concatenate([ix[s] for s in range(n_expert)], axis=1)
        info_c = info_r.T
        gate_up = jnp.dot(tx[...], w_all[x, :, : 2 * hidden], preferred_element_type=F32)
        back = jnp.dot(ox[...], w_all[x, :, 2 * hidden :], preferred_element_type=F32)
        gate = jnp.where(info_c[:, 0:1] == expert, info_c[:, 4:5], 0.0) + jnp.where(
            info_c[:, 2:3] == expert, info_c[:, 5:6], 0.0
        )
        act_grad = back * gate
        gate_pre, up_pre = gate_up[:, :hidden], gate_up[:, hidden:]
        s = jax.nn.sigmoid(gate_pre)
        gate_grad = act_grad * up_pre * s * (1.0 + gate_pre * (1.0 - s))
        up_grad = act_grad * (gate_pre * s)
        grad = jnp.concatenate([gate_grad, up_grad], axis=1).astype(BF16)
        grad_s[...] = grad
        pick = picker(
            info_r[0:1, :], info_r[1:2, :], info_r[2:3, :], info_r[3:4, :], expert, n_expert, rows
        )
        hid[x, d, :used, :] = jnp.dot(pick, grad, preferred_element_type=F32).astype(BF16)
        for i, (low, high) in enumerate(groups):
            if x == high - 1:
                grads.step(i, 0)
        across = (((1,), (1,)), ((), ()))
        for j in range(1, n_expert):
            target = lax.rem(e + j, n_expert)
            there = ix[target]
            rank = lax.broadcasted_iota(jnp.int32, (48, rows), 0).astype(F32)
            hit0 = jnp.logical_and(there[0:1] == expert, there[1:2] == rank)
            hit1 = jnp.logical_and(there[2:3] == expert, there[3:4] == rank)
            take = jnp.where(jnp.logical_or(hit0, hit1), 1.0, 0.0).astype(BF16)
            theirs = grad_s[pl.ds(pl.multiple_of(target * rows, rows), rows), :]
            few = jnp.dot(take, theirs, preferred_element_type=F32).astype(BF16)
            back = [
                lax.dot_general(
                    few, w_all[x, k * half : (k + 1) * half, : 2 * hidden], across,
                    preferred_element_type=F32,
                )[:CAP]
                for k in range(2)
            ]
            ret[target, x] = jnp.concatenate(back, axis=0).astype(BF16)
            sends.start(
                None,
                lambda j=j, target=target: remote(
                    ret.at[target, x], rx.at[e, x], r_s.at[x, j], r_r.at[x, j], target, d
                ),
            )
        ours = grad_s[pl.ds(pl.multiple_of(e * rows, rows), rows), :]
        for k in range(2):
            place = slice(k * half, (k + 1) * half)
            term = lax.dot_general(
                ours, w_all[x, place, : 2 * hidden], across, preferred_element_type=F32
            )
            acc[:, place] = term if x == 0 else acc[:, place] + term

    row = lax.broadcasted_iota(jnp.int32, (local_count * span, rows), 0)

    def reorder(s, fresh, d2, carry):
        joined = tt[s, d2]
        info = joined[width:].astype(F32).astype(jnp.int32)
        place0 = (info[0:1] - e * local_count) * span + info[1:2] + s * CAP
        place1 = (info[2:3] - e * local_count) * span + info[3:4] + s * CAP
        hit = jnp.logical_or(row == place0, row == place1)
        pick = jnp.where(hit, 1.0, 0.0).astype(BF16)
        got = lax.dot_general(
            joined[:width], pick, (((1,), (1,)), ((), ())), preferred_element_type=F32
        ).astype(BF16)
        for x in range(local_count):
            place = pl.ds(pl.multiple_of(d2 * span, span), span)
            part = got[:, x * span : (x + 1) * span]
            slots[x, :, place] = part if fresh else slots[x, :, place] + part
        return carry

    count = n_data // 4
    stagger = 2
    lag = 2
    turns = stagger * last + count + lag + 1
    hooks = {t: [] for t in range(turns)}
    hooks[0].append(prepare)
    hooks[2].append(spread)
    hooks[min(6, turns - 1)].append(relay)
    hooks[min(7, turns - 1)].append(partners)
    for x in range(last):
        hooks[max(min(7 + x, turns - 1), stagger * x + count + lag)].append(functools.partial(compute, x))
    for t in range(turns):
        if t % stagger == 0 and 0 < t <= stagger * last:
            weights.step(t // stagger, 0)
        for x in range(local_count):
            if 0 < t - stagger * x < count:
                weights.step(x, t - stagger * x)
        for x in range(local_count):
            if 0 < t - stagger * x - lag <= count:
                weights.step_b(x, t - stagger * x - lag)
        for job in hooks[t]:
            job()
    compute(last)

    for s in range(1, count):
        for i in range(len(groups)):
            grads.step(i, s)
    for i in range(len(groups)):
        for s in range(1, count + 1):
            grads.step_b(i, s)
    for j in range(1, n_expert):
        source = lax.rem(e - j + n_expert, n_expert)
        remote(tt.at[source], tt.at[source], y_s.at[j], y_r.at[j], source, d).wait_recv()
        lax.fori_loop(0, n_data, functools.partial(reorder, source, False), 0)
    for i, (low, high) in enumerate(groups):
        grads.finish(i)
        for x in range(low, high):
            flat = hid[x].reshape(n_data * span, 2 * hidden)
            term = jnp.dot(slots[x], flat, preferred_element_type=F32) * scale
            out_g[x] = term[:, :hidden]
            out_u[x] = term[:, hidden:]
    mine_c = ix[e].T.astype(jnp.int32)
    lane = lax.broadcasted_iota(jnp.int32, (rows, local_count * 2 * CAP), 1)
    for j in range(1, n_expert):
        source = lax.rem(e - j + n_expert, n_expert)
        for x in range(local_count):
            remote(
                ret.at[e, x], rx.at[source, x], r_s.at[x, j], r_r.at[x, j], source, d
            ).wait_recv()
        first = source * local_count
        place0 = (mine_c[:, 0:1] - first) * (2 * CAP) + mine_c[:, 1:2]
        place1 = (mine_c[:, 2:3] - first) * (2 * CAP) + mine_c[:, 3:4]
        came = rx[source].reshape(local_count * 2 * CAP, half)
        for k in range(2):
            hit = jnp.logical_or(lane == place0 + k * CAP, lane == place1 + k * CAP)
            put = jnp.where(hit, 1.0, 0.0).astype(BF16)
            acc[:, k * half : (k + 1) * half] += jnp.dot(put, came, preferred_element_type=F32)
    tg[...] = acc[...].astype(BF16)
    sends.finish()


def picker(e0, p0, e1, p1, expert, n_expert, rows):
    shape = (n_expert * CAP, n_expert * rows)
    slot = lax.broadcasted_iota(jnp.int32, shape, 0)
    base = (lax.broadcasted_iota(jnp.int32, (1, shape[1]), 1) // rows) * CAP
    want0 = jnp.where(e0 == expert, p0.astype(jnp.int32) + base, -1)
    want1 = jnp.where(e1 == expert, p1.astype(jnp.int32) + base, -1)
    hit = jnp.logical_or(slot == want0, slot == want1)
    return jnp.where(hit, 1.0, 0.0).astype(BF16)


def local(tokens, out_grad, routes, gates, w_gate, w_up, w_down_t):
    rows, model = tokens.shape
    n_expert = lax.axis_size("expert")
    n_data = lax.axis_size("dp")
    local_count, width, hidden = w_gate.shape
    count = n_data // 4
    any_, vmem = pl.BlockSpec(memory_space=pl.ANY), pl.BlockSpec(memory_space=pltpu.VMEM)
    dma = pltpu.SemaphoreType.DMA
    total, span = n_expert * rows, -(-n_expert * CAP // 128) * 128

    def chain_sems(number):
        return [
            dma((number, count)), dma((number, count)), dma((number, count)),
            dma((number, 2 * count)), dma((number, n_data)),
        ]

    shape = jax.ShapeDtypeStruct
    return pl.pallas_call(
        functools.partial(
            fused_kernel, n_expert, n_data, 1.0 / math.sqrt(rows * n_expert * n_data)
        ),
        out_shape=(
            shape((rows, model), BF16),
            shape((local_count, width, hidden), F32),
            shape((local_count, width, hidden), F32),
        ),
        in_specs=[any_, any_, vmem, vmem, any_, any_, any_],
        out_specs=[vmem] * 3,
        scratch_shapes=[
            pltpu.VMEM((local_count, model, 3 * hidden), BF16),
            pltpu.VMEM((total, model), BF16),
            pltpu.VMEM((total, model), BF16),
            pltpu.VMEM((n_expert, 8, rows), F32),
            pltpu.VMEM((n_data, width + INFO, rows), BF16),
            pltpu.VMEM((n_expert, n_data, width + INFO, rows), BF16),
            pltpu.VMEM((local_count, width, n_data * span), BF16),
            pltpu.VMEM((rows, model), F32),
            pltpu.VMEM((local_count, n_data, span, 2 * hidden), BF16),
            pltpu.VMEM((total, 2 * hidden), BF16),
            pltpu.VMEM((n_expert, local_count, 2 * CAP, model // 2), BF16),
            pltpu.VMEM((n_expert, local_count, 2 * CAP, model // 2), BF16),
            dma((5,)),
        ]
        + chain_sems(local_count)
        + chain_sems(min(2, local_count))
        + [
            dma((3, n_expert)), dma((3, n_expert)), dma((n_data,)), dma((n_data,)),
            dma((n_expert,)), dma((n_expert,)),
            dma((local_count, n_expert)), dma((local_count, n_expert)),
        ],
        compiler_params=pltpu.CompilerParams(
            collective_id=0, has_side_effects=True, vmem_limit_bytes=60 * 1024 * 1024
        ),
    )(tokens, out_grad, routes.T, gates.T, w_gate, w_up, w_down_t)


def solution(mesh):
    row, split = P(("expert", "dp"), None), P("expert", "dp", None)
    return jax.shard_map(
        local,
        mesh=mesh,
        in_specs=(row, row, row, row, split, split, split),
        out_specs=(row, split, split),
        check_vma=False,
    )
```

```python
import functools
import math

import jax
import jax.numpy as jnp
from jax import lax
from jax.experimental import pallas as pl
from jax.experimental.pallas import tpu as pltpu
from jax.sharding import PartitionSpec as P

EXPERTS = 8
CAP = 40
INFO = 16
F32 = jnp.float32
BF16 = jnp.bfloat16


def remote(src, dst, send, recv, e, d):
    return pltpu.make_async_remote_copy(
        src_ref=src,
        dst_ref=dst,
        send_sem=send,
        recv_sem=recv,
        device_id={"expert": e, "dp": d},
        device_id_type=pl.DeviceIdType.MESH,
    )


def when(cond, fn):
    if cond is None:
        fn()
    else:
        pl.when(cond)(fn)


class Sends:
    def __init__(self):
        self.items = []

    def start(self, cond, make):
        when(cond, lambda: make().start())
        self.items.append((cond, make))

    def finish(self):
        for cond, make in self.items:
            when(cond, lambda make=make: make().wait_send())


def column(q, b):
    return ((q // 2) * 2 + b) * 2 + lax.rem(q, 2)


def barrier(e, d, n_expert, n_data):
    sem = pltpu.get_barrier_semaphore()
    b, q, number = lax.rem(d // 2, 2), (d // 4) * 2 + lax.rem(d, 2), n_data // 2
    peers = [(e, column(lax.rem(q + j, number), b)) for j in range(1, number)]
    peers += [(e, column(q, 1 - b))]
    peers += [(lax.rem(e + j, n_expert), d) for j in range(1, n_expert)]
    for e2, d2 in peers:
        pl.semaphore_signal(
            sem,
            inc=1,
            device_id={"expert": e2, "dp": d2},
            device_id_type=pl.DeviceIdType.MESH,
        )
    pl.semaphore_wait(sem, len(peers))


def both(p, q):
    if p is None:
        return q
    return jnp.logical_and(p, q)


class Chain:
    def __init__(self, e, d, n_data, block, sems, sends, wide=True):
        self.e, self.block, self.sems, self.sends = e, block, sems, sends
        self.wide = wide
        self.count = n_data // 4
        self.abc = d // 4, lax.rem(d // 2, 2), lax.rem(d, 2)

    def index(self, a, b, c):
        return (a * 2 + b) * 2 + c

    def arrive(self, i, d2):
        block = self.block(i, d2)
        up_s, down_s, b_s, c_s, recv = self.sems
        remote(block, block, c_s.at[i, 0], recv.at[i, d2], self.e, self.index(*self.abc)).wait_recv()

    def send(self, cond, i, d2, target, sem):
        recv = self.sems[4]
        self.sends.start(
            cond,
            lambda: remote(self.block(i, d2), self.block(i, d2), sem, recv.at[i, d2], self.e, target),
        )

    def pass_on(self, cond, i, a2, up, down, slot):
        (a, b, c), index, count = self.abc, self.index, self.count
        up_s, down_s, b_s, c_s, _ = self.sems
        d2 = index(a2, b, c)
        if self.wide:
            self.send(cond, i, d2, index(a, 1 - b, c), b_s.at[i, a2])
        if up:
            self.send(both(cond, a < count - 1), i, d2, index(a + 1, b, c), up_s.at[i, slot])
        if down:
            self.send(both(cond, a > 0), i, d2, index(a - 1, b, c), down_s.at[i, slot])
        self.send(cond, i, d2, index(a, b, 1 - c), c_s.at[i, a2 * 2 + b])

    def from_b(self, cond, i, a2):
        a, b, c = self.abc
        d2 = self.index(a2, 1 - b, c)
        when(cond, lambda: self.arrive(i, d2))
        self.send(cond, i, d2, self.index(a, b, 1 - c), self.sems[3].at[i, a2 * 2 + 1 - b])

    def step(self, i, s):
        (a, b, c), count = self.abc, self.count
        if s == 0:
            self.pass_on(None, i, a, True, True, 0)
        elif s < count:
            for cond, a2, up in ((a >= s, a - s, True), (a + s < count, a + s, False)):
                d2 = self.index(a2, b, c)
                when(cond, lambda d2=d2: self.arrive(i, d2))
                self.pass_on(cond, i, a2, up, not up, s)

    def step_b(self, i, s):
        a, count = self.abc[0], self.count
        if s == 1:
            self.from_b(None, i, a)
        else:
            self.from_b(a >= s - 1, i, a - s + 1)
            self.from_b(a + s - 1 < count, i, a + s - 1)

    def finish(self, i):
        b, c = self.abc[1:]

        def one(j, carry):
            self.arrive(i, 2 * j + 1 - c if self.wide else self.index(j, b, 1 - c))
            return carry

        lax.fori_loop(0, (2 if self.wide else 1) * self.count, one, 0)


def fused_kernel(
    n_expert, n_data, scale, tok, og, routes, gates, w_g, w_u, w_dn,
    tg, out_g, out_u,
    w_all, tx, ox, ix, blocks, tt, slots, acc, hid, grad_s, ret, rx, off, on,
    own_sem, up_s, down_s, b_s, c_s, w_recv, hup_s, hdown_s, hb_s, hc_s, h_recv,
    x_s, x_r, t_s, t_r, y_s, y_r, r_s, r_r, p_s, p_r,
):
    e, d = lax.axis_index("expert"), lax.axis_index("dp")
    local_count, width, hidden = out_g.shape
    rows, model = tg.shape
    number = n_data // 2
    span = slots.shape[2] // number
    b, q = lax.rem(d // 2, 2), (d // 4) * 2 + lax.rem(d, 2)
    used = n_expert * CAP
    half = model // 2
    last = local_count - 1

    def w_block(i, d2):
        return w_all.at[i, pl.ds(d2 * width, width), :]


    def h_block(i, d2):
        return hid.at[i, (d2 // 4) * 2 + lax.rem(d2, 2), pl.ds(0, used), :]

    def mine(ref, e2):
        return ref.at[pl.ds(e2 * rows, rows), :]

    own = [
        pltpu.make_async_copy(
            w, w_all.at[:, pl.ds(d * width, width), pl.ds(i * hidden, hidden)], own_sem.at[i]
        )
        for i, w in enumerate((w_g, w_u, w_dn))
    ] + [
        pltpu.make_async_copy(tok, mine(tx, e), own_sem.at[3]),
        pltpu.make_async_copy(og, mine(ox, e), own_sem.at[4]),
    ]
    for copy in own:
        copy.start()
    barrier(e, d, n_expert, n_data)
    sends = Sends()
    weights = Chain(e, d, n_data, w_block, (up_s, down_s, b_s, c_s, w_recv), sends)
    grads = Chain(e, d, n_data, h_block, (hup_s, hdown_s, hb_s, hc_s, h_recv), sends, False)

    pairs = ((tok, tx, 0), (og, ox, 1))
    for j in range(1, n_expert):
        for src, dst, i in pairs:
            sends.start(
                None,
                lambda src=src, dst=dst, i=i, j=j: remote(
                    src, mine(dst, e), x_s.at[i, j], x_r.at[i, j], lax.rem(e + j, n_expert), d
                ),
            )
    for copy in own[:3]:
        copy.wait()
    for x in range(local_count):
        weights.step(x, 0)

    def prepare():
        e0, e1 = routes[0:1, :].astype(F32), routes[1:2, :].astype(F32)
        name = lax.broadcasted_iota(jnp.int32, (EXPERTS, rows), 0).astype(F32)
        hot0, hot1 = jnp.where(e0 == name, 1.0, 0.0), jnp.where(e1 == name, 1.0, 0.0)
        before = jnp.where(
            lax.broadcasted_iota(jnp.int32, (rows, rows), 0)
            < lax.broadcasted_iota(jnp.int32, (rows, rows), 1),
            1.0, 0.0,
        ).astype(BF16)
        seen = jnp.dot((hot0 + hot1).astype(BF16), before, preferred_element_type=F32)
        p0 = jnp.sum(seen * hot0, axis=0, keepdims=True)
        p1 = jnp.sum(seen * hot1, axis=0, keepdims=True)
        g = gates[...]
        info = jnp.concatenate([e0, p0, e1, p1, g, g], axis=0)
        ix[e] = info
        for j in range(1, n_expert):
            sends.start(
                None,
                lambda j=j: remote(
                    ix.at[e], ix.at[e], x_s.at[2, j], x_r.at[2, j], lax.rem(e + j, n_expert), d
                ),
            )
        side = jnp.concatenate([info, jnp.zeros_like(info)], axis=0).astype(BF16)
        own[3].wait()
        piece = 384
        for j in range(model // piece):
            part = tx[pl.ds(pl.multiple_of(e * rows, rows), rows), j * piece : (j + 1) * piece].T
            for k in range(piece // width):
                d2 = j * (piece // width) + k
                low = d2 // 2 % 2 * width
                blocks[d2 // 4 * 2 + d2 % 2, low : low + width, :] = part[k * width : (k + 1) * width]
        for j in range(number):
            blocks[j, 2 * width :, :] = side
        tt[e, q] = blocks[q]
        hid[:, :, used:, :] = jnp.zeros((local_count, number, span - used, 2 * hidden), BF16)

    def spread(part, parts):
        for j in range(1 + part, number, parts):
            q2 = lax.rem(q + j, number)
            sends.start(
                None,
                lambda j=j, q2=q2: remote(
                    blocks.at[q2], tt.at[e, q], t_s.at[j], t_r.at[j], e, column(q2, b)
                ),
            )

    def pass_slice(j):
        q2 = lax.rem(q - j + number, number)
        place = tt.at[e, q2]
        if j:
            remote(place, place, t_s.at[j], t_r.at[j], e, column(q2, b)).wait_recv()
        for k in range(1, n_expert):
            sends.start(
                None,
                lambda k=k, place=place: remote(
                    place, place, y_s.at[k, j], y_r.at[k, j], lax.rem(e + k, n_expert), d
                ),
            )

    def relay():
        for j in range(number):
            pass_slice(j)
        lax.fori_loop(0, number, functools.partial(reorder, e, True), 0)

    def partners():
        own[4].wait()
        for j in range(1, n_expert):
            source = lax.rem(e - j + n_expert, n_expert)
            for src, dst, i in pairs:
                remote(src, mine(dst, source), x_s.at[i, j], x_r.at[i, j], source, d).wait_recv()
            remote(ix.at[e], ix.at[source], x_s.at[2, j], x_r.at[2, j], source, d).wait_recv()

    def compute(x):
        weights.finish(x)
        expert = (e * local_count + x).astype(F32)
        info_r = jnp.concatenate([ix[s] for s in range(n_expert)], axis=1)
        info_c = info_r.T
        gate_up = jnp.dot(tx[...], w_all[x, :, : 2 * hidden], preferred_element_type=F32)
        back = jnp.dot(ox[...], w_all[x, :, 2 * hidden :], preferred_element_type=F32)
        gate = jnp.where(info_c[:, 0:1] == expert, info_c[:, 4:5], 0.0) + jnp.where(
            info_c[:, 2:3] == expert, info_c[:, 5:6], 0.0
        )
        act_grad = back * gate
        gate_pre, up_pre = gate_up[:, :hidden], gate_up[:, hidden:]
        s = jax.nn.sigmoid(gate_pre)
        gate_grad = act_grad * up_pre * s * (1.0 + gate_pre * (1.0 - s))
        up_grad = act_grad * (gate_pre * s)
        grad = jnp.concatenate([gate_grad, up_grad], axis=1).astype(BF16)
        grad_s[...] = grad
        pick = picker(
            info_r[0:1, :], info_r[1:2, :], info_r[2:3, :], info_r[3:4, :], expert, n_expert, rows
        )
        hid[x, q, :used, :] = jnp.dot(pick, grad, preferred_element_type=F32).astype(BF16)
        grads.step(x, 0)
        across = (((1,), (1,)), ((), ()))
        for j in range(1, n_expert):
            target = lax.rem(e + j, n_expert)
            there = ix[target]
            rank = lax.broadcasted_iota(jnp.int32, (48, rows), 0).astype(F32)
            hit0 = jnp.logical_and(there[0:1] == expert, there[1:2] == rank)
            hit1 = jnp.logical_and(there[2:3] == expert, there[3:4] == rank)
            take = jnp.where(jnp.logical_or(hit0, hit1), 1.0, 0.0).astype(BF16)
            theirs = grad_s[pl.ds(pl.multiple_of(target * rows, rows), rows), :]
            few = jnp.dot(take, theirs, preferred_element_type=F32).astype(BF16)
            back = [
                lax.dot_general(
                    few, w_all[x, k * half : (k + 1) * half, : 2 * hidden], across,
                    preferred_element_type=F32,
                )[:CAP]
                for k in range(2)
            ]
            ret[target, x] = jnp.concatenate(back, axis=0).astype(BF16)
            sends.start(
                None,
                lambda j=j, target=target: remote(
                    ret.at[target, x], rx.at[e, x], r_s.at[x, j], r_r.at[x, j], target, d
                ),
            )
        ours = grad_s[pl.ds(pl.multiple_of(e * rows, rows), rows), :]
        for k in range(2):
            place = slice(k * half, (k + 1) * half)
            term = lax.dot_general(
                ours, w_all[x, place, : 2 * hidden], across, preferred_element_type=F32
            )
            acc[:, place] = term if x == 0 else acc[:, place] + term

    row = lax.broadcasted_iota(jnp.int32, (local_count * span, rows), 0)

    def reorder(s, fresh, q2, carry):
        joined = tt[s, q2]
        info = joined[2 * width :].astype(F32).astype(jnp.int32)
        place0 = (info[0:1] - e * local_count) * span + info[1:2] + s * CAP
        place1 = (info[2:3] - e * local_count) * span + info[3:4] + s * CAP
        hit = jnp.logical_or(row == place0, row == place1)
        pick = jnp.where(hit, 1.0, 0.0).astype(BF16)
        got = lax.dot_general(
            joined[: 2 * width], pick, (((1,), (1,)), ((), ())), preferred_element_type=F32
        ).astype(BF16)
        for x in range(local_count):
            place = pl.ds(pl.multiple_of(q2 * span, span), span)
            part = got[:, x * span : (x + 1) * span]
            slots[x, :, place] = part if fresh else slots[x, :, place] + part
        return carry

    def over_y(x):
        return remote(off.at[x], on.at[x], p_s.at[x], p_r.at[x], e, column(q, 1 - b))

    def weight_grad(x):
        flat = hid[x].reshape(number * span, 2 * hidden)
        term = jnp.dot(slots[x], flat, preferred_element_type=F32) * scale
        low, high = term[:width], term[width:]
        keep = jnp.where(b == 0, low, high)
        off[x] = jnp.where(b == 0, high, low).astype(BF16)
        sends.start(None, lambda: over_y(x))
        out_g[x] = keep[:, :hidden]
        out_u[x] = keep[:, hidden:]

    def partners_slices():
        for j in range(1, n_expert):
            source = lax.rem(e - j + n_expert, n_expert)
            for k in range(number):
                place = tt.at[source, lax.rem(q - k + number, number)]
                remote(place, place, y_s.at[j, k], y_r.at[j, k], source, d).wait_recv()
            lax.fori_loop(0, number, functools.partial(reorder, source, False), 0)

    def put_back():
        mine_c = ix[e].T.astype(jnp.int32)
        lane = lax.broadcasted_iota(jnp.int32, (rows, local_count * 2 * CAP), 1)
        for j in range(1, n_expert):
            source = lax.rem(e - j + n_expert, n_expert)
            for x in range(local_count):
                remote(
                    ret.at[e, x], rx.at[source, x], r_s.at[x, j], r_r.at[x, j], source, d
                ).wait_recv()
            first = source * local_count
            place0 = (mine_c[:, 0:1] - first) * (2 * CAP) + mine_c[:, 1:2]
            place1 = (mine_c[:, 2:3] - first) * (2 * CAP) + mine_c[:, 3:4]
            came = rx[source].reshape(local_count * 2 * CAP, half)
            for k in range(2):
                hit = jnp.logical_or(lane == place0 + k * CAP, lane == place1 + k * CAP)
                put = jnp.where(hit, 1.0, 0.0).astype(BF16)
                acc[:, k * half : (k + 1) * half] += jnp.dot(put, came, preferred_element_type=F32)
        tg[...] = acc[...].astype(BF16)

    count = n_data // 4
    lag, begin, hand = 1, 1, 2
    prepare()
    for s in range(count - 1):
        for x in range(local_count):
            if s > 0:
                weights.step(x, s)
        for x in range(local_count):
            if s > lag:
                weights.step_b(x, s - lag)
        if s == min(begin, count - 2):
            spread(0, 1)
        if s == min(hand, count - 2):
            relay()
    partners()
    for k in range(local_count + count + 1):
        if k < local_count:
            weights.step(k, count - 1)
        if 0 < k <= local_count:
            for s in range(max(1, count - 1 - lag), count + 1):
                weights.step_b(k - 1, s)
            compute(k - 1)
        for x in range(local_count):
            s = k - 1 - x
            if 1 <= s < count:
                grads.step(x, s)
            if s == count:
                if x == 0:
                    partners_slices()
                if x == last:
                    put_back()
                grads.finish(x)
                weight_grad(x)
    for x in range(local_count):
        over_y(x).wait_recv()
        out_g[x] += on[x, :, :hidden].astype(F32)
        out_u[x] += on[x, :, hidden:].astype(F32)
    sends.finish()


def picker(e0, p0, e1, p1, expert, n_expert, rows):
    shape = (n_expert * CAP, n_expert * rows)
    slot = lax.broadcasted_iota(jnp.int32, shape, 0)
    base = (lax.broadcasted_iota(jnp.int32, (1, shape[1]), 1) // rows) * CAP
    want0 = jnp.where(e0 == expert, p0.astype(jnp.int32) + base, -1)
    want1 = jnp.where(e1 == expert, p1.astype(jnp.int32) + base, -1)
    hit = jnp.logical_or(slot == want0, slot == want1)
    return jnp.where(hit, 1.0, 0.0).astype(BF16)


def local(tokens, out_grad, routes, gates, w_gate, w_up, w_down_t):
    rows, model = tokens.shape
    n_expert = lax.axis_size("expert")
    n_data = lax.axis_size("dp")
    local_count, width, hidden = w_gate.shape
    count = n_data // 4
    any_, vmem = pl.BlockSpec(memory_space=pl.ANY), pl.BlockSpec(memory_space=pltpu.VMEM)
    dma = pltpu.SemaphoreType.DMA
    number = n_data // 2
    total, span = n_expert * rows, -(-n_expert * CAP // 128) * 128

    def chain_sems(number):
        return [
            dma((number, count)), dma((number, count)), dma((number, count)),
            dma((number, 2 * count)), dma((number, n_data)),
        ]

    shape = jax.ShapeDtypeStruct
    return pl.pallas_call(
        functools.partial(
            fused_kernel, n_expert, n_data, 1.0 / math.sqrt(rows * n_expert * n_data)
        ),
        out_shape=(
            shape((rows, model), BF16),
            shape((local_count, width, hidden), F32),
            shape((local_count, width, hidden), F32),
        ),
        in_specs=[any_, any_, vmem, vmem, any_, any_, any_],
        out_specs=[vmem] * 3,
        scratch_shapes=[
            pltpu.VMEM((local_count, model, 3 * hidden), BF16),
            pltpu.VMEM((total, model), BF16),
            pltpu.VMEM((total, model), BF16),
            pltpu.VMEM((n_expert, 8, rows), F32),
            pltpu.VMEM((number, 2 * width + INFO, rows), BF16),
            pltpu.VMEM((n_expert, number, 2 * width + INFO, rows), BF16),
            pltpu.VMEM((local_count, 2 * width, number * span), BF16),
            pltpu.VMEM((rows, model), F32),
            pltpu.VMEM((local_count, number, span, 2 * hidden), BF16),
            pltpu.VMEM((total, 2 * hidden), BF16),
            pltpu.VMEM((n_expert, local_count, 2 * CAP, model // 2), BF16),
            pltpu.VMEM((n_expert, local_count, 2 * CAP, model // 2), BF16),
            pltpu.VMEM((local_count, width, 2 * hidden), BF16),
            pltpu.VMEM((local_count, width, 2 * hidden), BF16),
            dma((5,)),
        ]
        + chain_sems(local_count)
        + chain_sems(local_count)
        + [
            dma((3, n_expert)), dma((3, n_expert)), dma((number,)), dma((number,)),
            dma((n_expert, number)), dma((n_expert, number)),
            dma((local_count, n_expert)), dma((local_count, n_expert)),
            dma((local_count,)), dma((local_count,)),
        ],
        compiler_params=pltpu.CompilerParams(
            collective_id=0, has_side_effects=True, vmem_limit_bytes=60 * 1024 * 1024
        ),
    )(tokens, out_grad, routes.T, gates.T, w_gate, w_up, w_down_t)


def solution(mesh):
    row, split = P(("expert", "dp"), None), P("expert", "dp", None)
    return jax.shard_map(
        local,
        mesh=mesh,
        in_specs=(row, row, row, row, split, split, split),
        out_specs=(row, split, split),
        check_vma=False,
    )
```

```python
import functools
import math

import jax
import jax.numpy as jnp
from jax import lax
from jax.experimental import pallas as pl
from jax.experimental.pallas import tpu as pltpu
from jax.sharding import PartitionSpec as P

EXPERTS = 8
CAP = 40
INFO = 16
PARTS = 4
F32 = jnp.float32
BF16 = jnp.bfloat16


def remote(src, dst, send, recv, e, d):
    return pltpu.make_async_remote_copy(
        src_ref=src,
        dst_ref=dst,
        send_sem=send,
        recv_sem=recv,
        device_id={"expert": e, "dp": d},
        device_id_type=pl.DeviceIdType.MESH,
    )


def when(cond, fn):
    if cond is None:
        fn()
    else:
        pl.when(cond)(fn)


class Sends:
    def __init__(self):
        self.items = []

    def start(self, cond, make):
        when(cond, lambda: make().start())
        self.items.append((cond, make))

    def finish(self):
        for cond, make in self.items:
            when(cond, lambda make=make: make().wait_send())


def column(q, b):
    return ((q // 2) * 2 + b) * 2 + lax.rem(q, 2)


def paired(q, m):
    for k in range(m.bit_length()):
        if m // 2**k % 2:
            q = q + 2**k * (1 - 2 * lax.rem(q // 2**k, 2))
    return q


def barrier(e, d, n_expert, n_data):
    sem = pltpu.get_barrier_semaphore()
    b, q, number = lax.rem(d // 2, 2), (d // 4) * 2 + lax.rem(d, 2), n_data // 2
    peers = [(e, column(lax.rem(q + j, number), b)) for j in range(1, number)]
    peers += [(e, column(q, 1 - b))]
    peers += [(lax.rem(e + j, n_expert), d) for j in range(1, n_expert)]
    for e2, d2 in peers:
        pl.semaphore_signal(
            sem,
            inc=1,
            device_id={"expert": e2, "dp": d2},
            device_id_type=pl.DeviceIdType.MESH,
        )
    pl.semaphore_wait(sem, len(peers))


def both(p, q):
    if p is None:
        return q
    return jnp.logical_and(p, q)


class Chain:
    def __init__(self, e, d, n_data, block, sems, sends, wide=True):
        self.e, self.block, self.sems, self.sends = e, block, sems, sends
        self.wide = wide
        self.count = n_data // 4
        self.abc = d // 4, lax.rem(d // 2, 2), lax.rem(d, 2)

    def index(self, a, b, c):
        return (a * 2 + b) * 2 + c

    def arrive(self, i, d2):
        block = self.block(i, d2)
        up_s, down_s, b_s, c_s, recv = self.sems
        remote(block, block, c_s.at[i, 0], recv.at[i, d2], self.e, self.index(*self.abc)).wait_recv()

    def send(self, cond, i, d2, target, sem):
        recv = self.sems[4]
        self.sends.start(
            cond,
            lambda: remote(self.block(i, d2), self.block(i, d2), sem, recv.at[i, d2], self.e, target),
        )

    def pass_on(self, cond, i, a2, up, down, slot):
        (a, b, c), index, count = self.abc, self.index, self.count
        up_s, down_s, b_s, c_s, _ = self.sems
        d2 = index(a2, b, c)
        if self.wide:
            self.send(cond, i, d2, index(a, 1 - b, c), b_s.at[i, a2])
        if up:
            self.send(both(cond, a < count - 1), i, d2, index(a + 1, b, c), up_s.at[i, slot])
        if down:
            self.send(both(cond, a > 0), i, d2, index(a - 1, b, c), down_s.at[i, slot])
        self.send(cond, i, d2, index(a, b, 1 - c), c_s.at[i, a2 * 2 + b])

    def from_b(self, cond, i, a2):
        a, b, c = self.abc
        d2 = self.index(a2, 1 - b, c)
        when(cond, lambda: self.arrive(i, d2))
        self.send(cond, i, d2, self.index(a, b, 1 - c), self.sems[3].at[i, a2 * 2 + 1 - b])

    def step(self, i, s):
        (a, b, c), count = self.abc, self.count
        if s == 0:
            self.pass_on(None, i, a, True, True, 0)
        elif s < count:
            for cond, a2, up in ((a >= s, a - s, True), (a + s < count, a + s, False)):
                d2 = self.index(a2, b, c)
                when(cond, lambda d2=d2: self.arrive(i, d2))
                self.pass_on(cond, i, a2, up, not up, s)

    def step_b(self, i, s):
        a, count = self.abc[0], self.count
        if s == 1:
            self.from_b(None, i, a)
        else:
            self.from_b(a >= s - 1, i, a - s + 1)
            self.from_b(a + s - 1 < count, i, a + s - 1)

    def finish(self, i):
        b, c = self.abc[1:]

        def one(j, carry):
            self.arrive(i, 2 * j + 1 - c if self.wide else self.index(j, b, 1 - c))
            return carry

        lax.fori_loop(0, (2 if self.wide else 1) * self.count, one, 0)


def fused_kernel(
    n_expert, n_data, scale, tok, og, routes, gates, w_g, w_u, w_dn,
    tg, out_g, out_u,
    w_all, tx, ox, ix, blocks, tt, slots, acc, hid, grad_s, ret, rx, off, on,
    own_sem, up_s, down_s, b_s, c_s, w_recv, hup_s, hdown_s, hb_s, hc_s, h_recv,
    x_s, x_r, t_s, t_r, y_s, y_r, r_s, r_r, p_s, p_r,
):
    e, d = lax.axis_index("expert"), lax.axis_index("dp")
    local_count, width, hidden = out_g.shape
    rows, model = tg.shape
    number = n_data // 2
    span = slots.shape[2] // number
    b, q = lax.rem(d // 2, 2), (d // 4) * 2 + lax.rem(d, 2)
    used = n_expert * CAP
    half = model // 2
    last = local_count - 1

    def w_block(i, d2):
        return w_all.at[i, pl.ds(d2 * width, width), :]


    def h_block(i, d2):
        return hid.at[i, (d2 // 4) * 2 + lax.rem(d2, 2), pl.ds(0, used), :]

    def mine(ref, e2):
        return ref.at[pl.ds(e2 * rows, rows), :]

    own = [
        pltpu.make_async_copy(
            w, w_all.at[:, pl.ds(d * width, width), pl.ds(i * hidden, hidden)], own_sem.at[i]
        )
        for i, w in enumerate((w_g, w_u, w_dn))
    ] + [
        pltpu.make_async_copy(tok, mine(tx, e), own_sem.at[3]),
        pltpu.make_async_copy(og, mine(ox, e), own_sem.at[4]),
    ]
    for copy in own:
        copy.start()
    barrier(e, d, n_expert, n_data)
    sends = Sends()
    weights = Chain(e, d, n_data, w_block, (up_s, down_s, b_s, c_s, w_recv), sends)
    grads = Chain(e, d, n_data, h_block, (hup_s, hdown_s, hb_s, hc_s, h_recv), sends, False)

    pairs = ((tok, tx, 0), (og, ox, 1))
    for j in range(1, n_expert):
        for src, dst, i in pairs:
            sends.start(
                None,
                lambda src=src, dst=dst, i=i, j=j: remote(
                    src, mine(dst, e), x_s.at[i, j], x_r.at[i, j], lax.rem(e + j, n_expert), d
                ),
            )
    for copy in own[:3]:
        copy.wait()
    for x in range(local_count):
        weights.step(x, 0)

    def prepare():
        e0, e1 = routes[0:1, :].astype(F32), routes[1:2, :].astype(F32)
        name = lax.broadcasted_iota(jnp.int32, (EXPERTS, rows), 0).astype(F32)
        hot0, hot1 = jnp.where(e0 == name, 1.0, 0.0), jnp.where(e1 == name, 1.0, 0.0)
        before = jnp.where(
            lax.broadcasted_iota(jnp.int32, (rows, rows), 0)
            < lax.broadcasted_iota(jnp.int32, (rows, rows), 1),
            1.0, 0.0,
        ).astype(BF16)
        seen = jnp.dot((hot0 + hot1).astype(BF16), before, preferred_element_type=F32)
        p0 = jnp.sum(seen * hot0, axis=0, keepdims=True)
        p1 = jnp.sum(seen * hot1, axis=0, keepdims=True)
        g = gates[...]
        info = jnp.concatenate([e0, p0, e1, p1, g, g], axis=0)
        ix[e] = info
        for j in range(1, n_expert):
            sends.start(
                None,
                lambda j=j: remote(
                    ix.at[e], ix.at[e], x_s.at[2, j], x_r.at[2, j], lax.rem(e + j, n_expert), d
                ),
            )
        side = jnp.concatenate([info, jnp.zeros_like(info)], axis=0).astype(BF16)
        own[3].wait()
        piece = 384
        for j in range(model // piece):
            part = tx[pl.ds(pl.multiple_of(e * rows, rows), rows), j * piece : (j + 1) * piece].T
            for k in range(piece // width):
                d2 = j * (piece // width) + k
                low = d2 // 2 % 2 * width
                blocks[d2 // 4 * 2 + d2 % 2, low : low + width, :] = part[k * width : (k + 1) * width]
        for j in range(number):
            blocks[j, 2 * width :, :] = side
        tt[e, q] = blocks[q]
        hid[:, :, used:, :] = jnp.zeros((local_count, number, span - used, 2 * hidden), BF16)

    def spread(part, parts):
        for j in range(1 + part, number, parts):
            q2 = paired(q, j)
            sends.start(
                None,
                lambda j=j, q2=q2: remote(
                    blocks.at[q2], tt.at[e, q], t_s.at[j], t_r.at[j], e, column(q2, b)
                ),
            )

    def pass_slice(j):
        q2 = paired(q, j)
        place = tt.at[e, q2]
        if j:
            remote(place, place, t_s.at[j], t_r.at[j], e, column(q2, b)).wait_recv()
        for k in range(1, n_expert):
            sends.start(
                None,
                lambda k=k, place=place: remote(
                    place, place, y_s.at[k, j], y_r.at[k, j], lax.rem(e + k, n_expert), d
                ),
            )

    def relay(low, high):
        for j in range(low, high):
            pass_slice(j)

    def partners():
        own[4].wait()
        for j in range(1, n_expert):
            source = lax.rem(e - j + n_expert, n_expert)
            for src, dst, i in pairs:
                remote(src, mine(dst, source), x_s.at[i, j], x_r.at[i, j], source, d).wait_recv()
            remote(ix.at[e], ix.at[source], x_s.at[2, j], x_r.at[2, j], source, d).wait_recv()

    def compute(x):
        weights.finish(x)
        expert = (e * local_count + x).astype(F32)
        info_r = jnp.concatenate([ix[s] for s in range(n_expert)], axis=1)
        info_c = info_r.T
        gate_up = jnp.dot(tx[...], w_all[x, :, : 2 * hidden], preferred_element_type=F32)
        back = jnp.dot(ox[...], w_all[x, :, 2 * hidden :], preferred_element_type=F32)
        gate = jnp.where(info_c[:, 0:1] == expert, info_c[:, 4:5], 0.0) + jnp.where(
            info_c[:, 2:3] == expert, info_c[:, 5:6], 0.0
        )
        act_grad = back * gate
        gate_pre, up_pre = gate_up[:, :hidden], gate_up[:, hidden:]
        s = jax.nn.sigmoid(gate_pre)
        gate_grad = act_grad * up_pre * s * (1.0 + gate_pre * (1.0 - s))
        up_grad = act_grad * (gate_pre * s)
        grad = jnp.concatenate([gate_grad, up_grad], axis=1).astype(BF16)
        grad_s[...] = grad
        pick = picker(
            info_r[0:1, :], info_r[1:2, :], info_r[2:3, :], info_r[3:4, :], expert, n_expert, rows
        )
        hid[x, q, :used, :] = jnp.dot(pick, grad, preferred_element_type=F32).astype(BF16)
        grads.step(x, 0)
        across = (((1,), (1,)), ((), ()))
        for j in range(1, n_expert):
            target = lax.rem(e + j, n_expert)
            there = ix[target]
            rank = lax.broadcasted_iota(jnp.int32, (48, rows), 0).astype(F32)
            hit0 = jnp.logical_and(there[0:1] == expert, there[1:2] == rank)
            hit1 = jnp.logical_and(there[2:3] == expert, there[3:4] == rank)
            take = jnp.where(jnp.logical_or(hit0, hit1), 1.0, 0.0).astype(BF16)
            theirs = grad_s[pl.ds(pl.multiple_of(target * rows, rows), rows), :]
            few = jnp.dot(take, theirs, preferred_element_type=F32).astype(BF16)
            back = [
                lax.dot_general(
                    few, w_all[x, k * half : (k + 1) * half, : 2 * hidden], across,
                    preferred_element_type=F32,
                )[:CAP]
                for k in range(2)
            ]
            ret[target, x] = jnp.concatenate(back, axis=0).astype(BF16)
            sends.start(
                None,
                lambda j=j, target=target: remote(
                    ret.at[target, x], rx.at[e, x], r_s.at[x, j], r_r.at[x, j], target, d
                ),
            )
        ours = grad_s[pl.ds(pl.multiple_of(e * rows, rows), rows), :]
        for k in range(2):
            place = slice(k * half, (k + 1) * half)
            term = lax.dot_general(
                ours, w_all[x, place, : 2 * hidden], across, preferred_element_type=F32
            )
            acc[:, place] = term if x == 0 else acc[:, place] + term

    row = lax.broadcasted_iota(jnp.int32, (local_count * span, rows), 0)

    def reorder(s, fresh, q2, carry):
        joined = tt[s, q2]
        info = joined[2 * width :].astype(F32).astype(jnp.int32)
        place0 = (info[0:1] - e * local_count) * span + info[1:2] + s * CAP
        place1 = (info[2:3] - e * local_count) * span + info[3:4] + s * CAP
        hit = jnp.logical_or(row == place0, row == place1)
        pick = jnp.where(hit, 1.0, 0.0).astype(BF16)
        got = lax.dot_general(
            joined[: 2 * width], pick, (((1,), (1,)), ((), ())), preferred_element_type=F32
        ).astype(BF16)
        for x in range(local_count):
            place = pl.ds(pl.multiple_of(q2 * span, span), span)
            part = got[:, x * span : (x + 1) * span]
            slots[x, :, place] = part if fresh else slots[x, :, place] + part
        return carry

    def over_y(x):
        return remote(off.at[x], on.at[x], p_s.at[x], p_r.at[x], e, column(q, 1 - b))

    def weight_grad(x):
        flat = hid[x].reshape(number * span, 2 * hidden)
        term = jnp.dot(slots[x], flat, preferred_element_type=F32) * scale
        low, high = term[:width], term[width:]
        keep = jnp.where(b == 0, low, high)
        off[x] = jnp.where(b == 0, high, low).astype(BF16)
        sends.start(None, lambda: over_y(x))
        out_g[x] = keep[:, :hidden]
        out_u[x] = keep[:, hidden:]

    def partners_slices():
        for j in range(1, n_expert):
            source = lax.rem(e - j + n_expert, n_expert)
            for k in range(number):
                place = tt.at[source, paired(q, k)]
                remote(place, place, y_s.at[j, k], y_r.at[j, k], source, d).wait_recv()
            lax.fori_loop(0, number, functools.partial(reorder, source, False), 0)

    def put_back():
        mine_c = ix[e].T.astype(jnp.int32)
        lane = lax.broadcasted_iota(jnp.int32, (rows, local_count * 2 * CAP), 1)
        for j in range(1, n_expert):
            source = lax.rem(e - j + n_expert, n_expert)
            for x in range(local_count):
                remote(
                    ret.at[e, x], rx.at[source, x], r_s.at[x, j], r_r.at[x, j], source, d
                ).wait_recv()
            first = source * local_count
            place0 = (mine_c[:, 0:1] - first) * (2 * CAP) + mine_c[:, 1:2]
            place1 = (mine_c[:, 2:3] - first) * (2 * CAP) + mine_c[:, 3:4]
            came = rx[source].reshape(local_count * 2 * CAP, half)
            for k in range(2):
                hit = jnp.logical_or(lane == place0 + k * CAP, lane == place1 + k * CAP)
                put = jnp.where(hit, 1.0, 0.0).astype(BF16)
                acc[:, k * half : (k + 1) * half] += jnp.dot(put, came, preferred_element_type=F32)
        tg[...] = acc[...].astype(BF16)

    count = n_data // 4
    lag, begin, hand, sort = 1, 0, (0, 4, number), local_count
    prepare()
    for s in range(count - 1):
        for x in range(local_count):
            if s > 0:
                weights.step(x, s)
        for x in range(local_count):
            if s > lag:
                weights.step_b(x, s - lag)
        if s == min(begin, count - 2):
            spread(0, 1)
        if s < len(hand):
            relay(hand[s - 1] if s else 0, hand[s])
    for k in range(local_count + count + 1):
        if k < local_count:
            weights.step(k, count - 1)
        if k == sort:
            lax.fori_loop(0, number, functools.partial(reorder, e, True), 0)
        if k == 1:
            partners()
        if 0 < k <= local_count:
            for s in range(max(1, count - 1 - lag), count + 1):
                weights.step_b(k - 1, s)
            compute(k - 1)
        for x in range(local_count):
            s = k - 1 - x
            if 1 <= s < count:
                grads.step(x, s)
            if s == count:
                if x == 0:
                    partners_slices()
                if x == last:
                    put_back()
                grads.finish(x)
                weight_grad(x)
    for x in range(local_count):
        over_y(x).wait_recv()
        out_g[x] += on[x, :, :hidden].astype(F32)
        out_u[x] += on[x, :, hidden:].astype(F32)
    sends.finish()


def picker(e0, p0, e1, p1, expert, n_expert, rows):
    shape = (n_expert * CAP, n_expert * rows)
    slot = lax.broadcasted_iota(jnp.int32, shape, 0)
    base = (lax.broadcasted_iota(jnp.int32, (1, shape[1]), 1) // rows) * CAP
    want0 = jnp.where(e0 == expert, p0.astype(jnp.int32) + base, -1)
    want1 = jnp.where(e1 == expert, p1.astype(jnp.int32) + base, -1)
    hit = jnp.logical_or(slot == want0, slot == want1)
    return jnp.where(hit, 1.0, 0.0).astype(BF16)


def hand_over(*refs):
    came, went = refs[9:]
    work = []
    for i in range(3):
        size = refs[i].shape[0] // PARTS if refs[i].shape[0] % PARTS == 0 else refs[i].shape[0]
        for k in range(refs[i].shape[0] // size):
            part, n = pl.ds(k * size, size), i * PARTS + k
            held = refs[6 + i].at[part]
            work.append(
                (
                    pltpu.make_async_copy(refs[i].at[part], held, came.at[n]),
                    pltpu.make_async_copy(held, refs[3 + i].at[part], went.at[n]),
                )
            )
    for first, _ in work:
        first.start()
    for first, then in work:
        first.wait()
        then.start()
    for _, then in work:
        then.wait()


def local(tokens, out_grad, routes, gates, w_gate, w_up, w_down_t):
    rows, model = tokens.shape
    n_expert = lax.axis_size("expert")
    n_data = lax.axis_size("dp")
    local_count, width, hidden = w_gate.shape
    count = n_data // 4
    any_, vmem = pl.BlockSpec(memory_space=pl.ANY), pl.BlockSpec(memory_space=pltpu.VMEM)
    dma = pltpu.SemaphoreType.DMA
    number = n_data // 2
    total, span = n_expert * rows, -(-n_expert * CAP // 128) * 128

    def chain_sems(number):
        return [
            dma((number, count)), dma((number, count)), dma((number, count)),
            dma((number, 2 * count)), dma((number, n_data)),
        ]

    shape = jax.ShapeDtypeStruct
    results = pl.pallas_call(
        functools.partial(
            fused_kernel, n_expert, n_data, 1.0 / math.sqrt(rows * n_expert * n_data)
        ),
        out_shape=(
            shape((rows, model), BF16),
            shape((local_count, width, hidden), F32),
            shape((local_count, width, hidden), F32),
        ),
        in_specs=[any_, any_, vmem, vmem, any_, any_, any_],
        out_specs=[vmem] * 3,
        scratch_shapes=[
            pltpu.VMEM((local_count, model, 3 * hidden), BF16),
            pltpu.VMEM((total, model), BF16),
            pltpu.VMEM((total, model), BF16),
            pltpu.VMEM((n_expert, 8, rows), F32),
            pltpu.VMEM((number, 2 * width + INFO, rows), BF16),
            pltpu.VMEM((n_expert, number, 2 * width + INFO, rows), BF16),
            pltpu.VMEM((local_count, 2 * width, number * span), BF16),
            pltpu.VMEM((rows, model), F32),
            pltpu.VMEM((local_count, number, span, 2 * hidden), BF16),
            pltpu.VMEM((total, 2 * hidden), BF16),
            pltpu.VMEM((n_expert, local_count, 2 * CAP, model // 2), BF16),
            pltpu.VMEM((n_expert, local_count, 2 * CAP, model // 2), BF16),
            pltpu.VMEM((local_count, width, 2 * hidden), BF16),
            pltpu.VMEM((local_count, width, 2 * hidden), BF16),
            dma((5,)),
        ]
        + chain_sems(local_count)
        + chain_sems(local_count)
        + [
            dma((3, n_expert)), dma((3, n_expert)), dma((number,)), dma((number,)),
            dma((n_expert, number)), dma((n_expert, number)),
            dma((local_count, n_expert)), dma((local_count, n_expert)),
            dma((local_count,)), dma((local_count,)),
        ],
        compiler_params=pltpu.CompilerParams(
            collective_id=0, has_side_effects=True, vmem_limit_bytes=60 * 1024 * 1024
        ),
    )(tokens, out_grad, routes.T, gates.T, w_gate, w_up, w_down_t)
    return pl.pallas_call(
        hand_over,
        out_shape=tuple(shape(r.shape, r.dtype) for r in results),
        in_specs=[any_] * 3,
        out_specs=[any_] * 3,
        scratch_shapes=[pltpu.VMEM(r.shape, r.dtype) for r in results]
        + [dma((3 * PARTS,)), dma((3 * PARTS,))],
    )(*results)


def solution(mesh):
    row, split = P(("expert", "dp"), None), P("expert", "dp", None)
    return jax.shard_map(
        local,
        mesh=mesh,
        in_specs=(row, row, row, row, split, split, split),
        out_specs=(row, split, split),
        check_vma=False,
    )
```

```python
import functools
import math

import jax
import jax.numpy as jnp
from jax import lax
from jax.experimental import pallas as pl
from jax.experimental.pallas import tpu as pltpu
from jax.sharding import PartitionSpec as P

EXPERTS = 8
CAP = 40
INFO = 16
PARTS = 4
F32 = jnp.float32
BF16 = jnp.bfloat16


def remote(src, dst, send, recv, e, d):
    return pltpu.make_async_remote_copy(
        src_ref=src,
        dst_ref=dst,
        send_sem=send,
        recv_sem=recv,
        device_id={"expert": e, "dp": d},
        device_id_type=pl.DeviceIdType.MESH,
    )


def when(cond, fn):
    if cond is None:
        fn()
    else:
        pl.when(cond)(fn)


class Sends:
    def __init__(self):
        self.items = []

    def start(self, cond, make):
        when(cond, lambda: make().start())
        self.items.append((cond, make))

    def finish(self):
        for cond, make in self.items:
            when(cond, lambda make=make: make().wait_send())


def column(q, b):
    return ((q // 2) * 2 + b) * 2 + lax.rem(q, 2)


def paired(q, m):
    for k in range(m.bit_length()):
        if m // 2**k % 2:
            q = q + 2**k * (1 - 2 * lax.rem(q // 2**k, 2))
    return q


def barrier(e, d, n_expert, n_data, meanwhile):
    sem = pltpu.get_barrier_semaphore()
    b, q, number = lax.rem(d // 2, 2), (d // 4) * 2 + lax.rem(d, 2), n_data // 2
    peers = [(e, column(lax.rem(q + j, number), b)) for j in range(1, number)]
    peers += [(e, column(q, 1 - b))]
    peers += [(lax.rem(e + j, n_expert), d) for j in range(1, n_expert)]
    for e2, d2 in peers:
        pl.semaphore_signal(
            sem,
            inc=1,
            device_id={"expert": e2, "dp": d2},
            device_id_type=pl.DeviceIdType.MESH,
        )
    meanwhile()
    pl.semaphore_wait(sem, len(peers))


def both(p, q):
    if p is None:
        return q
    return jnp.logical_and(p, q)


class Chain:
    def __init__(self, e, d, n_data, block, sems, sends, wide=True):
        self.e, self.block, self.sems, self.sends = e, block, sems, sends
        self.wide = wide
        self.count = n_data // 4
        self.abc = d // 4, lax.rem(d // 2, 2), lax.rem(d, 2)

    def index(self, a, b, c):
        return (a * 2 + b) * 2 + c

    def arrive(self, i, d2):
        block = self.block(i, d2)
        up_s, down_s, b_s, c_s, recv = self.sems
        remote(block, block, c_s.at[i, 0], recv.at[i, d2], self.e, self.index(*self.abc)).wait_recv()

    def send(self, cond, i, d2, target, sem):
        recv = self.sems[4]
        self.sends.start(
            cond,
            lambda: remote(self.block(i, d2), self.block(i, d2), sem, recv.at[i, d2], self.e, target),
        )

    def pass_on(self, cond, i, a2, up, down, slot):
        (a, b, c), index, count = self.abc, self.index, self.count
        up_s, down_s, b_s, c_s, _ = self.sems
        d2 = index(a2, b, c)
        if self.wide:
            self.send(cond, i, d2, index(a, 1 - b, c), b_s.at[i, a2])
        if up:
            self.send(both(cond, a < count - 1), i, d2, index(a + 1, b, c), up_s.at[i, slot])
        if down:
            self.send(both(cond, a > 0), i, d2, index(a - 1, b, c), down_s.at[i, slot])
        self.send(cond, i, d2, index(a, b, 1 - c), c_s.at[i, a2 * 2 + b])

    def from_b(self, cond, i, a2):
        a, b, c = self.abc
        d2 = self.index(a2, 1 - b, c)
        when(cond, lambda: self.arrive(i, d2))
        self.send(cond, i, d2, self.index(a, b, 1 - c), self.sems[3].at[i, a2 * 2 + 1 - b])

    def step(self, i, s):
        (a, b, c), count = self.abc, self.count
        if s == 0:
            self.pass_on(None, i, a, True, True, 0)
        elif s < count:
            for cond, a2, up in ((a >= s, a - s, True), (a + s < count, a + s, False)):
                d2 = self.index(a2, b, c)
                when(cond, lambda d2=d2: self.arrive(i, d2))
                self.pass_on(cond, i, a2, up, not up, s)

    def step_b(self, i, s):
        a, count = self.abc[0], self.count
        if s == 1:
            self.from_b(None, i, a)
        else:
            self.from_b(a >= s - 1, i, a - s + 1)
            self.from_b(a + s - 1 < count, i, a + s - 1)

    def finish(self, i):
        b, c = self.abc[1:]

        def one(j, carry):
            self.arrive(i, 2 * j + 1 - c if self.wide else self.index(j, b, 1 - c))
            return carry

        lax.fori_loop(0, (2 if self.wide else 1) * self.count, one, 0)


def fused_kernel(
    n_expert, n_data, scale, tok, og, routes, gates, w_g, w_u, w_dn,
    tg, out_g, out_u,
    w_all, tx, ox, ix, blocks, tt, slots, acc, hid, grad_s, ret, rx, off, on,
    own_sem, up_s, down_s, b_s, c_s, w_recv, hup_s, hdown_s, hb_s, hc_s, h_recv,
    x_s, x_r, t_s, t_r, y_s, y_r, r_s, r_r, p_s, p_r,
):
    e, d = lax.axis_index("expert"), lax.axis_index("dp")
    local_count, width, hidden = out_g.shape
    rows, model = tg.shape
    number = n_data // 2
    span = slots.shape[2] // number
    b, q = lax.rem(d // 2, 2), (d // 4) * 2 + lax.rem(d, 2)
    used = n_expert * CAP
    half = model // 2
    last = local_count - 1

    def w_block(i, d2):
        return w_all.at[i, pl.ds(d2 * width, width), :]


    def h_block(i, d2):
        return hid.at[i, (d2 // 4) * 2 + lax.rem(d2, 2), pl.ds(0, used), :]

    def mine(ref, e2):
        return ref.at[pl.ds(e2 * rows, rows), :]

    own = [
        pltpu.make_async_copy(
            w, w_all.at[:, pl.ds(d * width, width), pl.ds(i * hidden, hidden)], own_sem.at[i]
        )
        for i, w in enumerate((w_g, w_u, w_dn))
    ] + [
        pltpu.make_async_copy(tok, mine(tx, e), own_sem.at[3]),
        pltpu.make_async_copy(og, mine(ox, e), own_sem.at[4]),
    ]
    for copy in own:
        copy.start()

    def clear():
        hid[:, :, used:, :] = jnp.zeros((local_count, number, span - used, 2 * hidden), BF16)

    barrier(e, d, n_expert, n_data, clear)
    sends = Sends()
    weights = Chain(e, d, n_data, w_block, (up_s, down_s, b_s, c_s, w_recv), sends)
    grads = Chain(e, d, n_data, h_block, (hup_s, hdown_s, hb_s, hc_s, h_recv), sends, False)

    pairs = ((tok, tx, 0), (og, ox, 1))
    for j in range(1, n_expert):
        for src, dst, i in pairs:
            sends.start(
                None,
                lambda src=src, dst=dst, i=i, j=j: remote(
                    src, mine(dst, e), x_s.at[i, j], x_r.at[i, j], lax.rem(e + j, n_expert), d
                ),
            )
    for copy in own[:3]:
        copy.wait()
    for x in range(local_count):
        weights.step(x, 0)

    def prepare():
        e0, e1 = routes[0:1, :].astype(F32), routes[1:2, :].astype(F32)
        name = lax.broadcasted_iota(jnp.int32, (EXPERTS, rows), 0).astype(F32)
        hot0, hot1 = jnp.where(e0 == name, 1.0, 0.0), jnp.where(e1 == name, 1.0, 0.0)
        before = jnp.where(
            lax.broadcasted_iota(jnp.int32, (rows, rows), 0)
            < lax.broadcasted_iota(jnp.int32, (rows, rows), 1),
            1.0, 0.0,
        ).astype(BF16)
        seen = jnp.dot((hot0 + hot1).astype(BF16), before, preferred_element_type=F32)
        p0 = jnp.sum(seen * hot0, axis=0, keepdims=True)
        p1 = jnp.sum(seen * hot1, axis=0, keepdims=True)
        g = gates[...]
        info = jnp.concatenate([e0, p0, e1, p1, g, g], axis=0)
        ix[e] = info
        for j in range(1, n_expert):
            sends.start(
                None,
                lambda j=j: remote(
                    ix.at[e], ix.at[e], x_s.at[2, j], x_r.at[2, j], lax.rem(e + j, n_expert), d
                ),
            )
        side = jnp.concatenate([info, jnp.zeros_like(info)], axis=0).astype(BF16)
        own[3].wait()
        piece = 384
        for j in range(model // piece):
            part = tx[pl.ds(pl.multiple_of(e * rows, rows), rows), j * piece : (j + 1) * piece].T
            for k in range(piece // width):
                d2 = j * (piece // width) + k
                low = d2 // 2 % 2 * width
                blocks[d2 // 4 * 2 + d2 % 2, low : low + width, :] = part[k * width : (k + 1) * width]
        for j in range(number):
            blocks[j, 2 * width :, :] = side
        tt[e, q] = blocks[q]

    def spread(part, parts):
        for j in range(1 + part, number, parts):
            q2 = paired(q, j)
            sends.start(
                None,
                lambda j=j, q2=q2: remote(
                    blocks.at[q2], tt.at[e, q], t_s.at[j], t_r.at[j], e, column(q2, b)
                ),
            )

    def pass_slice(j):
        q2 = paired(q, j)
        place = tt.at[e, q2]
        if j:
            remote(place, place, t_s.at[j], t_r.at[j], e, column(q2, b)).wait_recv()
        for k in range(1, n_expert):
            sends.start(
                None,
                lambda k=k, place=place: remote(
                    place, place, y_s.at[k, j], y_r.at[k, j], lax.rem(e + k, n_expert), d
                ),
            )

    def relay(low, high):
        for j in range(low, high):
            pass_slice(j)

    def partners():
        own[4].wait()
        for j in range(1, n_expert):
            source = lax.rem(e - j + n_expert, n_expert)
            for src, dst, i in pairs:
                remote(src, mine(dst, source), x_s.at[i, j], x_r.at[i, j], source, d).wait_recv()
            remote(ix.at[e], ix.at[source], x_s.at[2, j], x_r.at[2, j], source, d).wait_recv()

    def compute(x):
        weights.finish(x)
        expert = (e * local_count + x).astype(F32)
        info_r = jnp.concatenate([ix[s] for s in range(n_expert)], axis=1)
        info_c = info_r.T
        gate_up = jnp.dot(tx[...], w_all[x, :, : 2 * hidden], preferred_element_type=F32)
        back = jnp.dot(ox[...], w_all[x, :, 2 * hidden :], preferred_element_type=F32)
        gate = jnp.where(info_c[:, 0:1] == expert, info_c[:, 4:5], 0.0) + jnp.where(
            info_c[:, 2:3] == expert, info_c[:, 5:6], 0.0
        )
        act_grad = back * gate
        gate_pre, up_pre = gate_up[:, :hidden], gate_up[:, hidden:]
        s = jax.nn.sigmoid(gate_pre)
        gate_grad = act_grad * up_pre * s * (1.0 + gate_pre * (1.0 - s))
        up_grad = act_grad * (gate_pre * s)
        grad = jnp.concatenate([gate_grad, up_grad], axis=1).astype(BF16)
        grad_s[...] = grad
        pick = picker(
            info_r[0:1, :], info_r[1:2, :], info_r[2:3, :], info_r[3:4, :], expert, n_expert, rows
        )
        hid[x, q, :used, :] = jnp.dot(pick, grad, preferred_element_type=F32).astype(BF16)
        grads.step(x, 0)
        across = (((1,), (1,)), ((), ()))
        for j in range(1, n_expert):
            target = lax.rem(e + j, n_expert)
            there = ix[target]
            rank = lax.broadcasted_iota(jnp.int32, (48, rows), 0).astype(F32)
            hit0 = jnp.logical_and(there[0:1] == expert, there[1:2] == rank)
            hit1 = jnp.logical_and(there[2:3] == expert, there[3:4] == rank)
            take = jnp.where(jnp.logical_or(hit0, hit1), 1.0, 0.0).astype(BF16)
            theirs = grad_s[pl.ds(pl.multiple_of(target * rows, rows), rows), :]
            few = jnp.dot(take, theirs, preferred_element_type=F32).astype(BF16)
            back = [
                lax.dot_general(
                    few, w_all[x, k * half : (k + 1) * half, : 2 * hidden], across,
                    preferred_element_type=F32,
                )[:CAP]
                for k in range(2)
            ]
            ret[target, x] = jnp.concatenate(back, axis=0).astype(BF16)
            sends.start(
                None,
                lambda j=j, target=target: remote(
                    ret.at[target, x], rx.at[e, x], r_s.at[x, j], r_r.at[x, j], target, d
                ),
            )
        ours = grad_s[pl.ds(pl.multiple_of(e * rows, rows), rows), :]
        for k in range(2):
            place = slice(k * half, (k + 1) * half)
            term = lax.dot_general(
                ours, w_all[x, place, : 2 * hidden], across, preferred_element_type=F32
            )
            acc[:, place] = term if x == 0 else acc[:, place] + term

    row = lax.broadcasted_iota(jnp.int32, (local_count * span, rows), 0)

    def reorder(s, fresh, q2, carry):
        joined = tt[s, q2]
        info = joined[2 * width :].astype(F32).astype(jnp.int32)
        place0 = (info[0:1] - e * local_count) * span + info[1:2] + s * CAP
        place1 = (info[2:3] - e * local_count) * span + info[3:4] + s * CAP
        hit = jnp.logical_or(row == place0, row == place1)
        pick = jnp.where(hit, 1.0, 0.0).astype(BF16)
        got = lax.dot_general(
            joined[: 2 * width], pick, (((1,), (1,)), ((), ())), preferred_element_type=F32
        ).astype(BF16)
        for x in range(local_count):
            place = pl.ds(pl.multiple_of(q2 * span, span), span)
            part = got[:, x * span : (x + 1) * span]
            slots[x, :, place] = part if fresh else slots[x, :, place] + part
        return carry

    def over_y(x):
        return remote(off.at[x], on.at[x], p_s.at[x], p_r.at[x], e, column(q, 1 - b))

    def weight_grad(x):
        flat = hid[x].reshape(number * span, 2 * hidden)
        term = jnp.dot(slots[x], flat, preferred_element_type=F32) * scale
        low, high = term[:width], term[width:]
        keep = jnp.where(b == 0, low, high)
        off[x] = jnp.where(b == 0, high, low).astype(BF16)
        sends.start(None, lambda: over_y(x))
        out_g[x] = keep[:, :hidden]
        out_u[x] = keep[:, hidden:]

    def partners_slices():
        for j in range(1, n_expert):
            source = lax.rem(e - j + n_expert, n_expert)
            for k in range(number):
                place = tt.at[source, paired(q, k)]
                remote(place, place, y_s.at[j, k], y_r.at[j, k], source, d).wait_recv()
            lax.fori_loop(0, number, functools.partial(reorder, source, False), 0)

    def put_back():
        mine_c = ix[e].T.astype(jnp.int32)
        lane = lax.broadcasted_iota(jnp.int32, (rows, local_count * 2 * CAP), 1)
        for j in range(1, n_expert):
            source = lax.rem(e - j + n_expert, n_expert)
            for x in range(local_count):
                remote(
                    ret.at[e, x], rx.at[source, x], r_s.at[x, j], r_r.at[x, j], source, d
                ).wait_recv()
            first = source * local_count
            place0 = (mine_c[:, 0:1] - first) * (2 * CAP) + mine_c[:, 1:2]
            place1 = (mine_c[:, 2:3] - first) * (2 * CAP) + mine_c[:, 3:4]
            came = rx[source].reshape(local_count * 2 * CAP, half)
            for k in range(2):
                hit = jnp.logical_or(lane == place0 + k * CAP, lane == place1 + k * CAP)
                put = jnp.where(hit, 1.0, 0.0).astype(BF16)
                acc[:, k * half : (k + 1) * half] += jnp.dot(put, came, preferred_element_type=F32)
        tg[...] = acc[...].astype(BF16)

    count = n_data // 4
    lag, begin, hand, sort = 1, 0, (0, 4, number), local_count
    prepare()
    for s in range(count - 1):
        for x in range(local_count):
            if s > 0:
                weights.step(x, s)
        for x in range(local_count):
            if s > lag:
                weights.step_b(x, s - lag)
        if s == min(begin, count - 2):
            spread(0, 1)
        if s < len(hand):
            relay(hand[s - 1] if s else 0, hand[s])
    for k in range(local_count + count + 1):
        if k < local_count:
            weights.step(k, count - 1)
        if k == sort:
            lax.fori_loop(0, number, functools.partial(reorder, e, True), 0)
        if k == 1:
            partners()
        if 0 < k <= local_count:
            for s in range(max(1, count - 1 - lag), count + 1):
                weights.step_b(k - 1, s)
            compute(k - 1)
        for x in range(local_count):
            s = k - 1 - x
            if 1 <= s < count:
                grads.step(x, s)
            if s == count:
                if x == 0:
                    partners_slices()
                if x == last:
                    put_back()
                grads.finish(x)
                weight_grad(x)
    for x in range(local_count):
        over_y(x).wait_recv()
        out_g[x] += on[x, :, :hidden].astype(F32)
        out_u[x] += on[x, :, hidden:].astype(F32)
    sends.finish()


def picker(e0, p0, e1, p1, expert, n_expert, rows):
    shape = (n_expert * CAP, n_expert * rows)
    slot = lax.broadcasted_iota(jnp.int32, shape, 0)
    base = (lax.broadcasted_iota(jnp.int32, (1, shape[1]), 1) // rows) * CAP
    want0 = jnp.where(e0 == expert, p0.astype(jnp.int32) + base, -1)
    want1 = jnp.where(e1 == expert, p1.astype(jnp.int32) + base, -1)
    hit = jnp.logical_or(slot == want0, slot == want1)
    return jnp.where(hit, 1.0, 0.0).astype(BF16)


def hand_over(*refs):
    came, went = refs[9:]
    work = []
    for i in range(3):
        size = refs[i].shape[0] // PARTS if refs[i].shape[0] % PARTS == 0 else refs[i].shape[0]
        for k in range(refs[i].shape[0] // size):
            part, n = pl.ds(k * size, size), i * PARTS + k
            held = refs[6 + i].at[part]
            work.append(
                (
                    pltpu.make_async_copy(refs[i].at[part], held, came.at[n]),
                    pltpu.make_async_copy(held, refs[3 + i].at[part], went.at[n]),
                )
            )
    for first, _ in work:
        first.start()
    for first, then in work:
        first.wait()
        then.start()
    for _, then in work:
        then.wait()


def local(tokens, out_grad, routes, gates, w_gate, w_up, w_down_t):
    rows, model = tokens.shape
    n_expert = lax.axis_size("expert")
    n_data = lax.axis_size("dp")
    local_count, width, hidden = w_gate.shape
    count = n_data // 4
    any_, vmem = pl.BlockSpec(memory_space=pl.ANY), pl.BlockSpec(memory_space=pltpu.VMEM)
    dma = pltpu.SemaphoreType.DMA
    number = n_data // 2
    total, span = n_expert * rows, -(-n_expert * CAP // 128) * 128

    def chain_sems(number):
        return [
            dma((number, count)), dma((number, count)), dma((number, count)),
            dma((number, 2 * count)), dma((number, n_data)),
        ]

    shape = jax.ShapeDtypeStruct
    results = pl.pallas_call(
        functools.partial(
            fused_kernel, n_expert, n_data, 1.0 / math.sqrt(rows * n_expert * n_data)
        ),
        out_shape=(
            shape((rows, model), BF16),
            shape((local_count, width, hidden), F32),
            shape((local_count, width, hidden), F32),
        ),
        in_specs=[any_, any_, vmem, vmem, any_, any_, any_],
        out_specs=[vmem] * 3,
        scratch_shapes=[
            pltpu.VMEM((local_count, model, 3 * hidden), BF16),
            pltpu.VMEM((total, model), BF16),
            pltpu.VMEM((total, model), BF16),
            pltpu.VMEM((n_expert, 8, rows), F32),
            pltpu.VMEM((number, 2 * width + INFO, rows), BF16),
            pltpu.VMEM((n_expert, number, 2 * width + INFO, rows), BF16),
            pltpu.VMEM((local_count, 2 * width, number * span), BF16),
            pltpu.VMEM((rows, model), F32),
            pltpu.VMEM((local_count, number, span, 2 * hidden), BF16),
            pltpu.VMEM((total, 2 * hidden), BF16),
            pltpu.VMEM((n_expert, local_count, 2 * CAP, model // 2), BF16),
            pltpu.VMEM((n_expert, local_count, 2 * CAP, model // 2), BF16),
            pltpu.VMEM((local_count, width, 2 * hidden), BF16),
            pltpu.VMEM((local_count, width, 2 * hidden), BF16),
            dma((5,)),
        ]
        + chain_sems(local_count)
        + chain_sems(local_count)
        + [
            dma((3, n_expert)), dma((3, n_expert)), dma((number,)), dma((number,)),
            dma((n_expert, number)), dma((n_expert, number)),
            dma((local_count, n_expert)), dma((local_count, n_expert)),
            dma((local_count,)), dma((local_count,)),
        ],
        compiler_params=pltpu.CompilerParams(
            collective_id=0, has_side_effects=True, vmem_limit_bytes=60 * 1024 * 1024
        ),
    )(tokens, out_grad, routes.T, gates.T, w_gate, w_up, w_down_t)
    return pl.pallas_call(
        hand_over,
        out_shape=tuple(shape(r.shape, r.dtype) for r in results),
        in_specs=[any_] * 3,
        out_specs=[any_] * 3,
        scratch_shapes=[pltpu.VMEM(r.shape, r.dtype) for r in results]
        + [dma((3 * PARTS,)), dma((3 * PARTS,))],
    )(*results)


def solution(mesh):
    row, split = P(("expert", "dp"), None), P("expert", "dp", None)
    return jax.shard_map(
        local,
        mesh=mesh,
        in_specs=(row, row, row, row, split, split, split),
        out_specs=(row, split, split),
        check_vma=False,
    )
```
